256 devices in a mesh: hel: 16 (over z_lo, x, core), rad: 16 (over z_hi, y).
Axes of the slice: x: 4, y: 4, z: 8 (z_hi: 4, z_lo: 2; z = z_hi * 2 + z_lo), core: 2. Of those that a mesh axis runs over, the one named last changes fastest.
Arguments:
- packet: bfloat16 [1024, 2, 64, 4, 512], P('rad', None, 'hel'), may hold values from -6 to 6
- first_propagator: bfloat16 [2, 1024, 1024], replicated, may hold values from -0.125 to 0.125
- second_propagator: bfloat16 [2, 512, 512], replicated, may hold values from -0.1875 to 0.1875
- potential: float32 [1024, 4, 512], P('rad'), may hold values from -3.140625 to 3.140625
- coupling: float32 [64, 4], replicated, may hold values from 0.2 to 0.8
- radial_weight: float32 [1024, 512], P('rad'), may hold values from 0.25 to 1
Outputs:
- advanced: bfloat16 [1024, 2, 64, 4, 512], P('rad', None, 'hel')
The draws below stay inside these ranges and needn't reach their ends.
All inputs are finite; a program needn't handle non-finite values.
Results may differ from the reference program's by a relative error of at most 0.007.
Values may be sent and summed in bfloat16 or wider, within the bound.
A program may use at most 128 MiB of HBM per device.

```python
import math
import jax
import jax.numpy as jnp
from jax import lax

R1 = 1024
R2 = 512
J = 4
K = 64


def steps_of(own_key, shape, shards, least, high):
    level = 1.0
    for position, shards_of in shards:
        steps = jax.random.uniform(jax.random.fold_in(jax.random.fold_in(own_key, 6), position), (shards_of,), jnp.float32, least / len(shards), high / len(shards))
        level = level * jnp.repeat(jnp.exp(steps), shape[position] // shards_of).reshape((-1,) + (1,) * (len(shape) - 1 - position))
    return level


def normal_values(rng, shape, deviation, bound, cuts=(), kind=jnp.bfloat16):
    gain = steps_of(rng, shape, cuts, -0.22, 0.18) if cuts else 1.0
    array = jax.random.normal(rng, shape, jnp.float32) * deviation * gain
    return jnp.minimum(jnp.maximum(array, -bound), bound).astype(kind)


def setup_inputs(seed: int = 0) -> dict:
    key_list = jax.random.split(jax.random.key(seed), 7)
    return {
        "packet": normal_values(key_list[0], (R1, 2, K, J, R2), 1.0, 6.0, ((0, 16), (2, 16))),
        "first_propagator": normal_values(key_list[1], (2, R1, R1), (2 * R1) ** -0.5, 0.125),
        "second_propagator": normal_values(key_list[2], (2, R2, R2), (2 * R2) ** -0.5, 0.1875),
        "potential": jnp.clip(jax.random.uniform(key_list[3], (R1, J, R2), jnp.float32, -3.140625, 3.140625), -3.140625, 3.140625),
        "coupling": jnp.clip(jax.random.uniform(key_list[4], (K, J), jnp.float32, 0.2, 0.8), 0.2, 0.8),
        "radial_weight": jnp.clip(jnp.exp(math.log(1.0) - 1.3862944 * jax.random.uniform(key_list[5], (R1, R2), jnp.float32) ** steps_of(key_list[5], (R1, R2), ((0, 16),), -0.2, 0.2)), 0.25, 1.0),
    }


def along_second(packet, propagator):
    width = propagator.shape[1]
    joined = jnp.concatenate([propagator[0], propagator[1]], axis=1).astype(jnp.float32)
    product = jnp.einsum("cjas,sq->cjaq", packet.astype(jnp.float32), joined)
    real_part = product[0, ..., :width] - product[1, ..., width:]
    imag_part = product[0, ..., width:] + product[1, ..., :width]
    return jnp.stack([real_part, imag_part]).astype(jnp.bfloat16)


def along_first(packet, propagator):
    width = propagator.shape[1]
    joined = jnp.concatenate([propagator[0], propagator[1]], axis=1).astype(jnp.float32)
    product = jnp.einsum("cjrs,rq->cjqs", packet.astype(jnp.float32), joined)
    real_part = product[0, :, :width, :] - product[1, :, width:, :]
    imag_part = product[0, :, width:, :] + product[1, :, :width, :]
    return jnp.stack([real_part, imag_part]).astype(jnp.bfloat16)


def reference(packet, first_propagator, second_propagator, potential, coupling, radial_weight):
    packet_old = jnp.transpose(packet, (1, 2, 3, 0, 4))
    angles = jnp.transpose(potential, (1, 0, 2))
    cosine = jnp.cos(angles)
    sine = jnp.sin(angles)
    count = packet_old.shape[1]

    def propagate(single):
        half = along_second(single, second_propagator)
        moved = along_first(half, first_propagator).astype(jnp.float32)
        phased = jnp.stack([moved[0] * cosine + moved[1] * sine, moved[1] * cosine - moved[0] * sine]).astype(jnp.bfloat16)
        return along_second(phased, second_propagator)

    kinetic = lax.map(propagate, jnp.moveaxis(packet_old, 1, 0))
    helicities = jnp.arange(count, dtype=jnp.int32)
    couple_up = jnp.where(helicities[:, None] < count - 1, coupling, 0.0)
    couple_down = jnp.concatenate([jnp.zeros((1, coupling.shape[1]), jnp.float32), coupling[:-1]], axis=0)

    def mix(helicity):
        current = lax.dynamic_index_in_dim(kinetic, helicity, 0, False).astype(jnp.float32)
        upper = lax.dynamic_index_in_dim(kinetic, jnp.minimum(helicity + 1, count - 1), 0, False).astype(jnp.float32)
        lower = lax.dynamic_index_in_dim(kinetic, jnp.maximum(helicity - 1, 0), 0, False).astype(jnp.float32)
        factor_up = lax.dynamic_index_in_dim(couple_up, helicity, 0, False)[None, :, None, None]
        factor_down = lax.dynamic_index_in_dim(couple_down, helicity, 0, False)[None, :, None, None]
        mixing = factor_up * upper + factor_down * lower
        real_part = current[0] + radial_weight * mixing[1]
        imag_part = current[1] - radial_weight * mixing[0]
        return jnp.stack([real_part, imag_part]).astype(jnp.bfloat16)

    advanced = lax.map(mix, helicities)
    return jnp.transpose(advanced, (3, 1, 0, 2, 4))
```

```python
import functools

import jax
import jax.numpy as jnp
from jax import lax
from jax.experimental import pallas as pl
from jax.experimental.pallas import tpu as pltpu
from jax.sharding import PartitionSpec as P

MESH = pl.DeviceIdType.MESH
BF16 = jnp.bfloat16
F32 = jnp.float32


def kernel(
    n_hel,
    n_rad,
    coup,
    pk,
    p1,
    p2,
    pot,
    rw,
    out,
    pkv,
    xs,
    p2v,
    pbig,
    p1v,
    p1t,
    potv,
    cosv,
    sinv,
    wv,
    fscr,
    hs,
    cols,
    ps,
    mv,
    ph,
    kin,
    outv,
    load_sem,
    pk_sem,
    out_sem,
    send1,
    recv1,
    send2,
    recv2,
    hsend,
    hrecv,
):
    kk = pkv.shape[0]
    h = lax.axis_index("hel")
    r = lax.axis_index("rad")
    partner = lax.rem(h + n_hel // 2, n_hel)
    zh, y = r // 4, lax.rem(r, 4)

    def order(i):
        return lax.rem(3 * i, 4)

    def peer(i):
        return lax.rem(zh + i, 4) * 4 + lax.rem(y + i // 4, 4)

    def load_packet(i):
        k = order(i)
        return [
            pltpu.make_async_copy(pk.at[:, c, k], pkv.at[k, c], pk_sem.at[i, c])
            for c in range(2)
        ]

    load_p2 = pltpu.make_async_copy(p2, p2v, load_sem.at[0])
    load_p1 = pltpu.make_async_copy(p1, p1v, load_sem.at[1])
    load_pot = pltpu.make_async_copy(pot, potv, load_sem.at[2])
    load_w = pltpu.make_async_copy(rw, wv, load_sem.at[3])
    load_p2.start()
    for i in range(kk):
        for copy in load_packet(i):
            copy.start()
    load_p1.start()
    load_pot.start()
    load_w.start()

    barrier = pltpu.get_barrier_semaphore()

    def greet(i, carry):
        pl.semaphore_signal(
            barrier, inc=1, device_id=(partner, peer(i)), device_id_type=MESH
        )
        return carry

    lax.fori_loop(0, n_rad, greet, 0)

    @pl.when(h > 0)
    def _():
        pl.semaphore_signal(barrier, inc=1, device_id=(h - 1, r), device_id_type=MESH)

    @pl.when(h < n_hel - 1)
    def _():
        pl.semaphore_signal(barrier, inc=1, device_id=(h + 1, r), device_id_type=MESH)

    load_p2.wait()
    for s in range(4):
        lanes = slice(s * 128, (s + 1) * 128)
        real, imag = p2v[0, :, lanes], p2v[1, :, lanes]
        pbig[:512, s * 256 : s * 256 + 128] = real
        pbig[:512, s * 256 + 128 : (s + 1) * 256] = imag
        pbig[512:, s * 256 : s * 256 + 128] = -imag
        pbig[512:, s * 256 + 128 : (s + 1) * 256] = real

    neighbours = jnp.where(h > 0, 1, 0) + jnp.where(h < n_hel - 1, 1, 0)
    pl.semaphore_wait(barrier, n_rad + neighbours)

    def first(i, carry):
        k = order(i)
        for copy in load_packet(i):
            copy.wait()
        for c in range(2):
            xs[:, c * 512 : (c + 1) * 512] = pkv[k, c].reshape(256, 512)
        for s in range(4):
            part = jnp.dot(
                xs[...],
                pbig[:, s * 256 : (s + 1) * 256],
                preferred_element_type=F32,
            )
            fscr[2 * s] = part[:, :128]
            fscr[2 * s + 1] = part[:, 128:]
        for j in range(4):
            for s in range(4):
                for c in range(2):
                    rows = fscr.at[2 * s + c][pl.ds(j, 64, stride=4), :]
                    hs[k, j * 4 + s, :, c * 128 : (c + 1) * 128] = rows.astype(BF16)

        def send(n, carry):
            p = peer(n)
            pltpu.make_async_remote_copy(
                src_ref=hs.at[k, p],
                dst_ref=cols.at[k, r],
                send_sem=send1.at[k],
                recv_sem=recv1.at[k],
                device_id=(partner, p),
                device_id_type=MESH,
            ).start()
            return carry

        lax.fori_loop(0, n_rad, send, 0)
        return carry

    lax.fori_loop(0, kk, first, 0)

    load_p1.wait()

    def flip(n, carry):
        rows = pl.ds(pl.multiple_of(n * 128, 128), 128)
        for c in range(2):
            p1t[c, rows, :] = p1v[c, :, rows].T
        return carry

    lax.fori_loop(0, 8, flip, 0)
    load_pot.wait()
    for s in range(4):
        fscr[s] = potv[:, :, s * 128 : (s + 1) * 128].reshape(256, 128)

    def phases(s, carry):
        for j in range(4):
            angle = fscr.at[s][pl.ds(j, 64, stride=4), :]
            cosv[j, s] = jnp.cos(angle)
            sinv[j, s] = jnp.sin(angle)
        return carry

    lax.fori_loop(0, 4, phases, 0)
    load_w.wait()

    def whole(src, dst, sems, i):
        return pltpu.make_async_remote_copy(
            src_ref=src.at[i],
            dst_ref=dst.at[i],
            send_sem=sems[0].at[i],
            recv_sem=sems[1].at[i],
            device_id=(partner, r),
            device_id_type=MESH,
        )

    def second(i, carry):
        k = order(i)
        whole(hs, cols, (send1, recv1), k).wait_recv()

        def block(n, carry):
            rows = pl.ds(pl.multiple_of(n * 256, 256), 256)
            u = cols[k].reshape(1024, 256)
            a = jnp.dot(p1t[0, rows, :], u, preferred_element_type=F32)
            b = jnp.dot(p1t[1, rows, :], u, preferred_element_type=F32)
            real = a[:, :128] - b[:, 128:]
            imag = a[:, 128:] + b[:, :128]
            four = pl.ds(n * 4, 4)
            ps[k, four, :, :128] = real.astype(BF16).reshape(4, 64, 128)
            ps[k, four, :, 128:] = imag.astype(BF16).reshape(4, 64, 128)
            return carry

        lax.fori_loop(0, 4, block, 0)

        def send(n, carry):
            p = peer(n)
            pltpu.make_async_remote_copy(
                src_ref=ps.at[k, p],
                dst_ref=mv.at[k, r],
                send_sem=send2.at[k],
                recv_sem=recv2.at[k],
                device_id=(partner, p),
                device_id_type=MESH,
            ).start()
            return carry

        lax.fori_loop(0, n_rad, send, 0)
        return carry

    lax.fori_loop(0, kk, second, 0)

    @pl.when(h == 0)
    def _():
        kin[0] = jnp.zeros_like(kin[0])

    @pl.when(h == n_hel - 1)
    def _():
        kin[kk + 1] = jnp.zeros_like(kin[kk + 1])

    def halo(k):
        low = k == 0
        return pltpu.make_async_remote_copy(
            src_ref=kin.at[1 if low else kk],
            dst_ref=kin.at[kk + 1 if low else 0],
            send_sem=hsend.at[0 if low else 1],
            recv_sem=hrecv.at[0 if low else 1],
            device_id=(h - 1 if low else h + 1, r),
            device_id_type=MESH,
        )

    def mix(k):
        g = h * kk + k
        last = n_hel * kk - 1
        for j in range(4):
            up = jnp.where(g < last, coup[g, j], 0.0)
            down = jnp.where(g > 0, coup[jnp.maximum(g - 1, 0), j], 0.0)
            rows = slice(j * 64, (j + 1) * 64)
            for s in range(4):
                re = slice(s * 256, s * 256 + 128)
                im = slice(s * 256 + 128, (s + 1) * 256)
                w = wv[:, s * 128 : (s + 1) * 128]
                mixed_im = up * kin[k + 2, rows, im].astype(F32) + down * kin[
                    k, rows, im
                ].astype(F32)
                mixed_re = up * kin[k + 2, rows, re].astype(F32) + down * kin[
                    k, rows, re
                ].astype(F32)
                place = pl.ds(j, 64, stride=4)
                fscr.at[s][place, :] = kin[k + 1, rows, re].astype(F32) + w * mixed_im
                fscr.at[4 + s][place, :] = (
                    kin[k + 1, rows, im].astype(F32) - w * mixed_re
                )
        for c in range(2):
            for s in range(4):
                outv[k, c, :, :, s * 128 : (s + 1) * 128] = (
                    fscr[4 * c + s].astype(BF16).reshape(64, 4, 128)
                )
        for c in range(2):
            pltpu.make_async_copy(
                outv.at[k, c], out.at[:, c, k], out_sem.at[k, c]
            ).start()

    def third(i, carry):
        k = order(i)
        whole(ps, mv, (send2, recv2), k).wait_recv()
        for j in range(4):
            rows = slice(j * 64, (j + 1) * 64)
            for s in range(4):
                re = mv[k, j * 4 + s, :, :128].astype(F32)
                im = mv[k, j * 4 + s, :, 128:].astype(F32)
                c, sn = cosv[j, s], sinv[j, s]
                ph[rows, s * 128 : (s + 1) * 128] = (re * c + im * sn).astype(BF16)
                ph[rows, 512 + s * 128 : 512 + (s + 1) * 128] = (
                    im * c - re * sn
                ).astype(BF16)
        for s in range(4):
            lanes = slice(s * 256, (s + 1) * 256)
            kin[k + 1, :, lanes] = jnp.dot(
                ph[...], pbig[:, lanes], preferred_element_type=F32
            ).astype(BF16)

        @pl.when((i == 0) & (h > 0))
        def _():
            halo(0).start()

        @pl.when((i == 1) & (h < n_hel - 1))
        def _():
            halo(kk - 1).start()

        @pl.when(i == 2)
        def _():
            @pl.when(h < n_hel - 1)
            def _():
                halo(0).wait_recv()

            mix(kk - 1)

        return carry

    lax.fori_loop(0, kk, third, 0)

    @pl.when(h > 0)
    def _():
        halo(kk - 1).wait_recv()

    def rest(k, carry):
        mix(k)
        return carry

    lax.fori_loop(0, kk - 1, rest, 0)

    def drain(k, carry):
        whole(hs, cols, (send1, recv1), k).wait_send()
        whole(ps, mv, (send2, recv2), k).wait_send()
        for c in range(2):
            pltpu.make_async_copy(outv.at[k, c], out.at[:, c, k], out_sem.at[k, c]).wait()
        return carry

    lax.fori_loop(0, kk, drain, 0)

    @pl.when(h > 0)
    def _():
        halo(0).wait_send()

    @pl.when(h < n_hel - 1)
    def _():
        halo(kk - 1).wait_send()


def solution(mesh):
    n_hel, n_rad = mesh.shape["hel"], mesh.shape["rad"]

    def per_device(packet, first, second, potential, coupling, weight):
        hbm = pl.BlockSpec(memory_space=pl.ANY)
        dma = pltpu.SemaphoreType.DMA
        return pl.pallas_call(
            functools.partial(kernel, n_hel, n_rad),
            out_shape=jax.ShapeDtypeStruct(packet.shape, BF16),
            in_specs=[pl.BlockSpec(memory_space=pltpu.SMEM)] + [hbm] * 5,
            out_specs=hbm,
            scratch_shapes=[
                pltpu.VMEM((4, 2, 64, 4, 512), BF16),
                pltpu.VMEM((256, 1024), BF16),
                pltpu.VMEM((2, 512, 512), BF16),
                pltpu.VMEM((1024, 1024), BF16),
                pltpu.VMEM((2, 1024, 1024), BF16),
                pltpu.VMEM((2, 1024, 1024), BF16),
                pltpu.VMEM((64, 4, 512), F32),
                pltpu.VMEM((4, 4, 64, 128), F32),
                pltpu.VMEM((4, 4, 64, 128), F32),
                pltpu.VMEM((64, 512), F32),
                pltpu.VMEM((8, 256, 128), F32),
                pltpu.VMEM((4, 16, 64, 256), BF16),
                pltpu.VMEM((4, 16, 64, 256), BF16),
                pltpu.VMEM((4, 16, 64, 256), BF16),
                pltpu.VMEM((4, 16, 64, 256), BF16),
                pltpu.VMEM((256, 1024), BF16),
                pltpu.VMEM((6, 256, 1024), BF16),
                pltpu.VMEM((4, 2, 64, 4, 512), BF16),
                dma((4,)),
                dma((4, 2)),
                dma((4, 2)),
                dma((4,)),
                dma((4,)),
                dma((4,)),
                dma((4,)),
                dma((2,)),
                dma((2,)),
            ],
            compiler_params=pltpu.CompilerParams(
                collective_id=0, has_side_effects=True
            ),
        )(coupling, packet, first, second, potential, weight)

    return jax.shard_map(
        per_device,
        mesh=mesh,
        in_specs=(
            P("rad", None, "hel", None, None),
            P(),
            P(),
            P("rad", None, None),
            P(),
            P("rad", None),
        ),
        out_specs=P("rad", None, "hel", None, None),
        check_vma=False,
    )
```

```python
import functools

import jax
import jax.numpy as jnp
from jax import lax
from jax.experimental import pallas as pl
from jax.experimental.pallas import tpu as pltpu
from jax.sharding import PartitionSpec as P

MESH = pl.DeviceIdType.MESH
BF16 = jnp.bfloat16
F32 = jnp.float32


def kernel(
    n_hel,
    n_rad,
    coup_hbm,
    pk,
    p1,
    p2,
    pot,
    rw,
    outv,
    pkv,
    xs,
    p2v,
    pbig,
    p1v,
    p1t,
    potv,
    cosv,
    sinv,
    wv,
    coup,
    fscr,
    hs,
    cols,
    ps,
    mv,
    ph,
    kin,
    relay,
    load_sem,
    pk_sem,
    send1,
    recv1,
    send2,
    recv2,
    hsend,
    hrecv,
    rsend,
    rrecv,
):
    kk = pkv.shape[0]
    h = lax.axis_index("hel")
    r = lax.axis_index("rad")
    middle = n_hel // 2
    partner = lax.rem(h + middle, n_hel)
    zh, y = r // 4, lax.rem(r, 4)
    z_lo = h // middle
    last_k = 1

    def order(i):
        return lax.rem(3 * i, 4)

    def peer(i):
        b = i // 4
        dy = jnp.where(b == 0, 2, jnp.where(b == 3, 0, 2 * b - 1))
        return lax.rem(zh + lax.rem(i, 4) + 1 + z_lo, 4) * 4 + lax.rem(y + dy, 4)

    is_low, is_high = h == middle - 1, h == middle
    carries_down = (h > middle + 1) & (lax.rem(h, 2) == 1)
    carries_up = (h < middle - 2) & (lax.rem(h, 2) == 1)

    barrier = pltpu.get_barrier_semaphore()

    def greet_one(target, rad):
        pl.semaphore_signal(
            barrier, inc=1, device_id=(target, rad), device_id_type=MESH
        )

    def greet(i, carry):
        greet_one(partner, peer(i))
        return carry

    lax.fori_loop(0, n_rad, greet, 0)

    @pl.when(h > 0)
    def _():
        greet_one(h - 1, r)

    @pl.when(h < n_hel - 1)
    def _():
        greet_one(h + 1, r)

    @pl.when(carries_down)
    def _():
        greet_one(middle, r)

    @pl.when(carries_up)
    def _():
        greet_one(middle - 1, r)

    @pl.when(is_low)
    def _():
        for q in range(1, 4):
            greet_one(middle + 2 * q + 1, r)

    @pl.when(is_high)
    def _():
        for q in range(3):
            greet_one(2 * q + 1, r)

    greeted = n_rad + jnp.where(h > 0, 1, 0) + jnp.where(h < n_hel - 1, 1, 0)
    greeted += jnp.where(is_low | is_high, 3, 0)
    greeted += jnp.where(carries_down | carries_up, 1, 0)

    def load_packet(i):
        k = order(i)
        return [
            pltpu.make_async_copy(pk.at[:, c, k], pkv.at[k, c], pk_sem.at[i, c])
            for c in range(2)
        ]

    load_p2 = pltpu.make_async_copy(p2, p2v, load_sem.at[0])
    load_p1 = pltpu.make_async_copy(p1, p1v, load_sem.at[1])
    load_pot = pltpu.make_async_copy(pot, potv, load_sem.at[2])
    load_w = pltpu.make_async_copy(rw, wv, load_sem.at[3])
    load_coup = pltpu.make_async_copy(coup_hbm, coup, load_sem.at[4])
    load_p2.start()
    for i in range(kk):
        for copy in load_packet(i):
            copy.start()
    load_p1.start()
    load_pot.start()
    load_w.start()
    load_coup.start()

    load_p2.wait()
    for s in range(4):
        lanes = slice(s * 128, (s + 1) * 128)
        real, imag = p2v[0, :, lanes], p2v[1, :, lanes]
        pbig[:512, s * 256 : s * 256 + 128] = real
        pbig[:512, s * 256 + 128 : (s + 1) * 256] = imag
        pbig[512:, s * 256 : s * 256 + 128] = -imag
        pbig[512:, s * 256 + 128 : (s + 1) * 256] = real

    def first(i, carry):
        k = order(i)
        for copy in load_packet(i):
            copy.wait()
        for c in range(2):
            xs[:, c * 512 : (c + 1) * 512] = pkv[k, c].reshape(256, 512)
        for s in range(4):
            part = jnp.dot(
                xs[...],
                pbig[:, s * 256 : (s + 1) * 256],
                preferred_element_type=F32,
            )
            fscr[2 * s] = part[:, :128]
            fscr[2 * s + 1] = part[:, 128:]
        for j in range(4):
            for s in range(4):
                for c in range(2):
                    rows = fscr.at[2 * s + c][pl.ds(j, 64, stride=4), :]
                    hs[k, j * 4 + s, :, c * 128 : (c + 1) * 128] = rows.astype(BF16)

        @pl.when(i == 0)
        def _():
            pl.semaphore_wait(barrier, greeted)

        def send(n, carry):
            p = peer(n)
            pltpu.make_async_remote_copy(
                src_ref=hs.at[k, p],
                dst_ref=cols.at[k, r],
                send_sem=send1.at[k],
                recv_sem=recv1.at[k],
                device_id=(partner, p),
                device_id_type=MESH,
            ).start()
            return carry

        lax.fori_loop(0, n_rad, send, 0)
        return carry

    lax.fori_loop(0, kk, first, 0)

    load_p1.wait()

    def flip(n, carry):
        rows = pl.ds(pl.multiple_of(n * 128, 128), 128)
        for c in range(2):
            p1t[c, rows, :] = p1v[c, :, rows].T
        return carry

    lax.fori_loop(0, 8, flip, 0)
    load_pot.wait()
    for s in range(4):
        fscr[s] = potv[:, :, s * 128 : (s + 1) * 128].reshape(256, 128)

    def phases(s, carry):
        for j in range(4):
            angle = fscr.at[s][pl.ds(j, 64, stride=4), :]
            cosv[j, s] = jnp.cos(angle)
            sinv[j, s] = jnp.sin(angle)
        return carry

    lax.fori_loop(0, 4, phases, 0)
    load_w.wait()
    load_coup.wait()

    def whole(src, dst, send_sem, recv_sem):
        return pltpu.make_async_remote_copy(
            src_ref=src,
            dst_ref=dst,
            send_sem=send_sem,
            recv_sem=recv_sem,
            device_id=(partner, r),
            device_id_type=MESH,
        )

    def all_first(k):
        return whole(hs.at[k], cols.at[k], send1.at[k], recv1.at[k])

    def all_second(k, base, rows, n):
        part = pl.ds(base, rows)
        return whole(
            ps.at[k, :, part], mv.at[k, :, part], send2.at[n], recv2.at[n]
        )

    def left(k):
        all_first(k).wait_recv()

        def block(n, carry):
            rows = pl.ds(pl.multiple_of(n * 256, 256), 256)
            u = cols[k].reshape(1024, 256)
            a = jnp.dot(p1t[0, rows, :], u, preferred_element_type=F32)
            b = jnp.dot(p1t[1, rows, :], u, preferred_element_type=F32)
            real = a[:, :128] - b[:, 128:]
            imag = a[:, 128:] + b[:, :128]
            four = pl.ds(n * 4, 4)
            ps[k, four, :, :128] = real.astype(BF16).reshape(4, 64, 128)
            ps[k, four, :, 128:] = imag.astype(BF16).reshape(4, 64, 128)
            return carry

        lax.fori_loop(0, 4, block, 0)

    def send_back(k, base, rows, n_sem):
        part = pl.ds(base, rows)

        def send(n, carry):
            p = peer(n)
            pltpu.make_async_remote_copy(
                src_ref=ps.at[k, p, part],
                dst_ref=mv.at[k, r, part],
                send_sem=send2.at[n_sem],
                recv_sem=recv2.at[n_sem],
                device_id=(partner, p),
                device_id_type=MESH,
            ).start()
            return carry

        lax.fori_loop(0, n_rad, send, 0)

    def second(i, carry):
        k = order(i)
        left(k)

        @pl.when(i < kk - 1)
        def _():
            send_back(k, 0, 64, i)

        @pl.when(i == kk - 1)
        def _():
            def part(n, carry):
                send_back(k, pl.multiple_of(n * 32, 32), 32, kk - 1 + n)
                return carry

            lax.fori_loop(0, 2, part, 0)

        return carry

    lax.fori_loop(0, kk, second, 0)

    @pl.when(h == 0)
    def _():
        kin[0] = jnp.zeros_like(kin[0])

    @pl.when(h == n_hel - 1)
    def _():
        kin[kk + 1] = jnp.zeros_like(kin[kk + 1])

    def ends(low):
        return (1, kk + 1, 0) if low else (kk, 0, 1)

    def halo(low):
        own, there, n = ends(low)
        return pltpu.make_async_remote_copy(
            src_ref=kin.at[own],
            dst_ref=kin.at[there],
            send_sem=hsend.at[n],
            recv_sem=hrecv.at[n],
            device_id=(h - 1 if low else h + 1, r),
            device_id_type=MESH,
        )

    def quarter(low, q, target, by_helper):
        own, there, n = ends(low)
        rows = pl.ds(q * 64, 64)
        return pltpu.make_async_remote_copy(
            src_ref=kin.at[own, rows],
            dst_ref=relay if by_helper else kin.at[there, rows],
            send_sem=hsend.at[n],
            recv_sem=rrecv if by_helper else hrecv.at[n],
            device_id=(target, r),
            device_id_type=MESH,
        )

    def hand_on(low):
        own, there, n = ends(low)
        q = (h - middle - 1) // 2 if low else (h - 1) // 2
        rows = pl.ds(pl.multiple_of(q * 64, 64), 64)
        return pltpu.make_async_remote_copy(
            src_ref=relay,
            dst_ref=kin.at[there, rows],
            send_sem=rsend,
            recv_sem=hrecv.at[n],
            device_id=(middle - 1 if low else middle, r),
            device_id_type=MESH,
        )

    def arrived_at_helper(low):
        return quarter(low, 0, partner, True)

    def mix(k, base, rows):
        g = h * kk + k
        last = n_hel * kk - 1
        for j in range(4):
            up = jnp.where(g < last, coup[j, g], 0.0)
            down = jnp.where(g > 0, coup[j, jnp.maximum(g - 1, 0)], 0.0)
            part = pl.ds(j * 64 + base, rows)
            for s in range(4):
                re = slice(s * 256, s * 256 + 128)
                im = slice(s * 256 + 128, (s + 1) * 256)
                w = wv[pl.ds(base, rows), s * 128 : (s + 1) * 128]
                mixed_im = up * kin[k + 2, part, im].astype(F32) + down * kin[
                    k, part, im
                ].astype(F32)
                mixed_re = up * kin[k + 2, part, re].astype(F32) + down * kin[
                    k, part, re
                ].astype(F32)
                place = pl.ds(j, rows, stride=4)
                fscr.at[s][place, :] = kin[k + 1, part, re].astype(F32) + w * mixed_im
                fscr.at[4 + s][place, :] = (
                    kin[k + 1, part, im].astype(F32) - w * mixed_re
                )
        for c in range(2):
            for s in range(4):
                outv[pl.ds(base, rows), c, k, :, s * 128 : (s + 1) * 128] = (
                    fscr[4 * c + s, : 4 * rows].astype(BF16).reshape(rows, 4, 128)
                )

    def finish(k, base, rows):
        part = pl.ds(base, rows)
        for j in range(4):
            place = slice(j * rows, (j + 1) * rows)
            for s in range(4):
                re = mv[k, j * 4 + s, part, :128].astype(F32)
                im = mv[k, j * 4 + s, part, 128:].astype(F32)
                c, sn = cosv[j, s, part], sinv[j, s, part]
                ph[place, s * 128 : (s + 1) * 128] = (re * c + im * sn).astype(BF16)
                ph[place, 512 + s * 128 : 512 + (s + 1) * 128] = (
                    im * c - re * sn
                ).astype(BF16)
        for s in range(4):
            lanes = slice(s * 256, (s + 1) * 256)
            result = jnp.dot(
                ph[: 4 * rows], pbig[:, lanes], preferred_element_type=F32
            ).astype(BF16)
            for j in range(4):
                kin[k + 1, pl.ds(j * 64 + base, rows), lanes] = result[
                    j * rows : (j + 1) * rows
                ]

    def third(i, carry):
        k = order(i)
        all_second(k, 0, 64, i).wait_recv()
        finish(k, 0, 64)

        @pl.when((i == 0) & (h > 0) & (h != middle))
        def _():
            halo(True).start()

        @pl.when((i == 1) & (h < n_hel - 1) & (h != middle - 1))
        def _():
            halo(False).start()

        @pl.when((i == 0) & is_high)
        def _():
            for q in range(1, 4):
                quarter(True, q, middle + 2 * q + 1, True).start()
            quarter(True, 0, middle - 1, False).start()

        @pl.when((i == 1) & is_low)
        def _():
            for q in range(3):
                quarter(False, q, 2 * q + 1, True).start()
            quarter(False, 3, middle, False).start()

        @pl.when((i == 1) & carries_down)
        def _():
            arrived_at_helper(True).wait_recv()
            hand_on(True).start()

        @pl.when((i == 2) & carries_up)
        def _():
            arrived_at_helper(False).wait_recv()
            hand_on(False).start()

        @pl.when((i == 2) & (h != middle - 1))
        def _():
            @pl.when(h < n_hel - 1)
            def _():
                halo(True).wait_recv()

            mix(kk - 1, 0, 64)

        return carry

    lax.fori_loop(0, kk - 1, third, 0)

    @pl.when((h > 0) & (h != middle))
    def _():
        halo(False).wait_recv()

    def ending(n, carry):
        base = pl.multiple_of(n * 32, 32)
        all_second(last_k, base, 32, kk - 1 + n).wait_recv()
        finish(last_k, base, 32)

        def rest(k, carry):
            mix(k, base, 32)
            return carry

        lax.fori_loop(jnp.where(is_high, 1, 0), kk - 1, rest, 0)
        return carry

    lax.fori_loop(0, 2, ending, 0)

    @pl.when(is_high)
    def _():
        halo(False).wait_recv()

    @pl.when(is_low)
    def _():
        halo(True).wait_recv()

    @pl.when(is_high | is_low)
    def _():
        mix(jnp.where(is_low, kk - 1, 0), 0, 64)

    def drain(i, carry):
        k = order(i)
        all_first(k).wait_send()

        @pl.when(i < kk - 1)
        def _():
            all_second(k, 0, 64, i).wait_send()

        return carry

    lax.fori_loop(0, kk, drain, 0)

    def drain_last(n, carry):
        base = pl.multiple_of(n * 32, 32)
        all_second(last_k, base, 32, kk - 1 + n).wait_send()
        return carry

    lax.fori_loop(0, 2, drain_last, 0)

    @pl.when(h > 0)
    def _():
        halo(True).wait_send()

    @pl.when(h < n_hel - 1)
    def _():
        halo(False).wait_send()

    @pl.when(carries_down)
    def _():
        hand_on(True).wait_send()

    @pl.when(carries_up)
    def _():
        hand_on(False).wait_send()


def solution(mesh):
    n_hel, n_rad = mesh.shape["hel"], mesh.shape["rad"]

    def per_device(packet, first, second, potential, coupling, weight):
        hbm = pl.BlockSpec(memory_space=pltpu.HBM)
        dma = pltpu.SemaphoreType.DMA
        return pl.pallas_call(
            functools.partial(kernel, n_hel, n_rad),
            out_shape=pltpu.VMEM(packet.shape, BF16),
            in_specs=[hbm] * 6,
            out_specs=pl.BlockSpec(memory_space=pltpu.VMEM),
            scratch_shapes=[
                pltpu.VMEM((4, 2, 64, 4, 512), BF16),
                pltpu.VMEM((256, 1024), BF16),
                pltpu.VMEM((2, 512, 512), BF16),
                pltpu.VMEM((1024, 1024), BF16),
                pltpu.VMEM((2, 1024, 1024), BF16),
                pltpu.VMEM((2, 1024, 1024), BF16),
                pltpu.VMEM((64, 4, 512), F32),
                pltpu.VMEM((4, 4, 64, 128), F32),
                pltpu.VMEM((4, 4, 64, 128), F32),
                pltpu.VMEM((64, 512), F32),
                pltpu.SMEM((4, 64), F32),
                pltpu.VMEM((8, 256, 128), F32),
                pltpu.VMEM((4, 16, 64, 256), BF16),
                pltpu.VMEM((4, 16, 64, 256), BF16),
                pltpu.VMEM((4, 16, 64, 256), BF16),
                pltpu.VMEM((4, 16, 64, 256), BF16),
                pltpu.VMEM((256, 1024), BF16),
                pltpu.VMEM((6, 256, 1024), BF16),
                pltpu.VMEM((64, 1024), BF16),
                dma((5,)),
                dma((4, 2)),
                dma((4,)),
                dma((4,)),
                dma((5,)),
                dma((5,)),
                dma((2,)),
                dma((2,)),
                dma,
                dma,
            ],
            compiler_params=pltpu.CompilerParams(
                collective_id=0,
                has_side_effects=True,
                vmem_limit_bytes=48 * 2**20,
            ),
        )(
            *(
                pltpu.with_memory_space_constraint(a, pltpu.HBM)
                for a in (coupling.T, packet, first, second, potential, weight)
            )
        )

    return jax.shard_map(
        per_device,
        mesh=mesh,
        in_specs=(
            P("rad", None, "hel", None, None),
            P(),
            P(),
            P("rad", None, None),
            P(),
            P("rad", None),
        ),
        out_specs=P("rad", None, "hel", None, None),
        check_vma=False,
    )
```

```python
import functools

import jax
import jax.numpy as jnp
from jax import lax
from jax.experimental import pallas as pl
from jax.experimental.pallas import tpu as pltpu
from jax.sharding import PartitionSpec as P

MESH = pl.DeviceIdType.MESH
BF16 = jnp.bfloat16
F32 = jnp.float32
HALF = 32


def place_of(j, s):
    return j * 4 + (s - j) % 4


def phase(moved, cosv, sinv, ph, base, count):
    here = slice(base, base + count)
    for j in range(4):
        rows = slice(j * count, (j + 1) * count)
        for s in range(4):
            p = place_of(j, s)
            re, im = moved[p, here, :128].astype(F32), moved[p, here, 128:].astype(F32)
            c, sn = cosv[j, s, here], sinv[j, s, here]
            ph[rows, s * 128 : (s + 1) * 128] = (re * c + im * sn).astype(BF16)
            ph[rows, 512 + s * 128 : 512 + (s + 1) * 128] = (im * c - re * sn).astype(
                BF16
            )


def propagate(ph, pbig, wide, count):
    for s in range(4):
        y = jnp.dot(
            ph[: 4 * count],
            pbig[:, s * 256 : (s + 1) * 256],
            preferred_element_type=F32,
        )
        for c in range(2):
            for j in range(4):
                wide.at[c][pl.ds(s * 4 + j, count, stride=16), :] = y[
                    j * count : (j + 1) * count, c * 128 : (c + 1) * 128
                ]


def combine(q, base, wide, part, wu, wd, res):
    new, rows = chunk(q), chunk(q, base)
    re = wide[0, new].astype(BF16).astype(F32)
    im = wide[1, new].astype(BF16).astype(F32)
    up, down = wu[rows], wd[rows]
    values = (
        (part[0, 0, rows] + up * im, part[0, 1, rows] - up * re),
        (part[1, 0, rows] + re, part[1, 1, rows] + im),
        (part[2, 0, rows] + down * im, part[2, 1, rows] - down * re),
    )
    for n in range(3):
        for c in range(2):
            res[n, c, pl.ds(pl.multiple_of(q * 16, 16), 16)] = (
                values[n][c].astype(BF16).reshape(16, 16, 128)
            )


def tiles(x):
    return x.astype(F32).reshape(32, 8, 128)


def flat(x):
    return x.reshape(256, 128)


def chunk(q, base=0):
    return pl.ds(pl.multiple_of(base + q * 256, 256), 256)


def last_rows(
    n_hel,
    early,
    done,
    pbig,
    moved,
    cosv,
    sinv,
    part,
    wu,
    wd,
    out,
    ph,
    wide,
    res,
    sems,
):
    z_lo = lax.axis_index("hel") // (n_hel // 2)
    low = 1 - z_lo

    def put_early(c):
        return pltpu.make_async_copy(early.at[c], out.at[:, c, 3 * z_lo], sems.at[12 + c])

    def put_done(n, c):
        return pltpu.make_async_copy(
            done.at[n, c], out.at[pl.ds(0, HALF), c, low + n], sems.at[14 + 2 * n + c]
        )

    def put_rows(q, n, c):
        return pltpu.make_async_copy(
            res.at[n, c, pl.ds(pl.multiple_of(q * 16, 16), 16)],
            out.at[pl.ds(pl.multiple_of(HALF + q * 16, 16), 16), c, low + n],
            sems.at[q * 6 + 2 * n + c],
        )

    for c in range(2):
        put_early(c).start()
        for n in range(3):
            put_done(n, c).start()
    phase(moved, cosv, sinv, ph, HALF, HALF)
    propagate(ph, pbig, wide, HALF)

    def block(q, carry):
        combine(q, HALF * 16, wide, part, wu, wd, res)
        for n in range(3):
            for c in range(2):
                put_rows(q, n, c).start()
        return carry

    lax.fori_loop(0, 2, block, 0)

    def drain(q, carry):
        for n in range(3):
            for c in range(2):
                put_rows(q, n, c).wait()
        return carry

    lax.fori_loop(0, 2, drain, 0)
    for c in range(2):
        put_early(c).wait()
        for n in range(3):
            put_done(n, c).wait()


def kernel(
    n_hel,
    n_rad,
    coup_hbm,
    pk,
    p1,
    p2,
    pot,
    rw,
    early,
    done,
    pbig,
    mvl,
    cosv,
    sinv,
    part,
    wu,
    wd,
    pkv,
    p2v,
    p1v,
    p1t,
    potv,
    wv,
    wr,
    coup,
    fscr,
    wide,
    hs,
    cols,
    ps,
    mv,
    ph,
    kin,
    relay,
    load_sem,
    pk_sem,
    send1,
    recv1,
    send2,
    recv2,
    hsend,
    hrecv,
    rsend,
    rrecv,
):
    kk = pkv.shape[0]
    h = lax.axis_index("hel")
    r = lax.axis_index("rad")
    middle = n_hel // 2
    partner = lax.rem(h + middle, n_hel)
    zh, y = r // 4, lax.rem(r, 4)
    z_lo = h // middle

    def order(i):
        return jnp.where(z_lo == 0, lax.rem(3 + i, 4), lax.rem(3 * i, 4))

    def peer(i):
        b = i // 4
        dy = jnp.where(b == 0, 2, jnp.where(b == 3, 0, 2 * b - 1))
        return lax.rem(zh + lax.rem(i, 4) + 1 + z_lo, 4) * 4 + lax.rem(y + dy, 4)

    is_low, is_high = h == middle - 1, h == middle
    carries_down = (h > middle + 1) & (lax.rem(h, 2) == 1)
    carries_up = (h < middle - 2) & (lax.rem(h, 2) == 1)

    barrier = pltpu.get_barrier_semaphore()

    def greet_one(target, rad):
        pl.semaphore_signal(
            barrier, inc=1, device_id=(target, rad), device_id_type=MESH
        )

    def greet(i, carry):
        greet_one(partner, peer(i))
        return carry

    lax.fori_loop(0, n_rad, greet, 0)

    @pl.when(h > 0)
    def _():
        greet_one(h - 1, r)

    @pl.when(h < n_hel - 1)
    def _():
        greet_one(h + 1, r)

    @pl.when(carries_down)
    def _():
        greet_one(middle, r)

    @pl.when(carries_up)
    def _():
        greet_one(middle - 1, r)

    @pl.when(is_low)
    def _():
        for q in range(1, 4):
            greet_one(middle + 2 * q + 1, r)

    @pl.when(is_high)
    def _():
        for q in range(3):
            greet_one(2 * q + 1, r)

    greeted = n_rad + jnp.where(h > 0, 1, 0) + jnp.where(h < n_hel - 1, 1, 0)
    greeted += jnp.where(is_low | is_high, 3, 0)
    greeted += jnp.where(carries_down | carries_up, 1, 0)

    def load_packet(i):
        k = order(i)
        return [
            pltpu.make_async_copy(pk.at[:, c, k], pkv.at[k, c], pk_sem.at[i, c])
            for c in range(2)
        ]

    load_p2 = pltpu.make_async_copy(p2, p2v, load_sem.at[0])
    load_p1 = pltpu.make_async_copy(p1, p1v, load_sem.at[1])
    load_pot = pltpu.make_async_copy(pot, potv, load_sem.at[2])
    load_w = pltpu.make_async_copy(rw, wv, load_sem.at[3])
    load_coup = pltpu.make_async_copy(coup_hbm, coup, load_sem.at[4])
    load_p2.start()
    for i in range(kk):
        for copy in load_packet(i):
            copy.start()
    load_p1.start()
    load_pot.start()
    load_w.start()
    load_coup.start()

    load_p2.wait()

    def first(i, carry):
        k = order(i)
        for copy in load_packet(i):
            copy.wait()
        x = [pkv[k, c].reshape(256, 512) for c in range(2)]
        for t in range(2):
            lanes = slice(t * 256, (t + 1) * 256)

            def product(c, d):
                return jnp.dot(x[c], p2v[d, :, lanes], preferred_element_type=F32)

            real = product(0, 0) - product(1, 1)
            imag = product(0, 1) + product(1, 0)
            for s in range(2):
                fscr[4 * t + 2 * s] = real[:, s * 128 : (s + 1) * 128]
                fscr[4 * t + 2 * s + 1] = imag[:, s * 128 : (s + 1) * 128]
            for j in range(4):
                for s in (2 * t, 2 * t + 1):
                    for c in range(2):
                        rows = fscr.at[2 * s + c][pl.ds(j, 64, stride=4), :]
                        hs[i, place_of(j, s), :, c * 128 : (c + 1) * 128] = rows.astype(
                            BF16
                        )

        @pl.when(i == 0)
        def _():
            pl.semaphore_wait(barrier, greeted)

        def send(n, carry):
            p = peer(n)
            pltpu.make_async_remote_copy(
                src_ref=hs.at[i, p],
                dst_ref=cols.at[i, r],
                send_sem=send1.at[i],
                recv_sem=recv1.at[i],
                device_id=(partner, p),
                device_id_type=MESH,
            ).start()
            return carry

        lax.fori_loop(0, n_rad, send, 0)
        return carry

    lax.fori_loop(0, kk, first, 0)

    for s in range(4):
        lanes = slice(s * 128, (s + 1) * 128)
        real, imag = p2v[0, :, lanes], p2v[1, :, lanes]
        pbig[:512, s * 256 : s * 256 + 128] = real
        pbig[:512, s * 256 + 128 : (s + 1) * 256] = imag
        pbig[512:, s * 256 : s * 256 + 128] = -imag
        pbig[512:, s * 256 + 128 : (s + 1) * 256] = real

    load_p1.wait()

    def flip(n, carry):
        rows = pl.ds(pl.multiple_of(n * 128, 128), 128)
        for c in range(2):
            p1t[c, rows, :] = p1v[c, :, rows].T
        return carry

    lax.fori_loop(0, 8, flip, 0)
    load_pot.wait()
    for s in range(4):
        fscr[s] = potv[:, :, s * 128 : (s + 1) * 128].reshape(256, 128)

    def phases(s, carry):
        for j in range(4):
            angle = fscr.at[s][pl.ds(j, 64, stride=4), :]
            cosv[j, s] = jnp.cos(angle)
            sinv[j, s] = jnp.sin(angle)
        return carry

    lax.fori_loop(0, 4, phases, 0)
    load_w.wait()
    load_coup.wait()
    for s in range(4):
        for j in range(4):
            wr[pl.ds(s * 4 + j, 64, stride=16), :] = wv[:, s * 128 : (s + 1) * 128]

    def whole(src, dst, send_sem, recv_sem):
        return pltpu.make_async_remote_copy(
            src_ref=src,
            dst_ref=dst,
            send_sem=send_sem,
            recv_sem=recv_sem,
            device_id=(partner, r),
            device_id_type=MESH,
        )

    def all_first(k):
        return whole(hs.at[k], cols.at[k], send1.at[k], recv1.at[k])

    def all_second(i):
        return whole(ps.at[i], mv.at[i], send2.at[i], recv2.at[i])

    def all_last(n):
        part = pl.ds(n * HALF, HALF)
        return whole(
            ps.at[3, :, part], mvl.at[:, part], send2.at[3 + n], recv2.at[3 + n]
        )

    def left(k):
        all_first(k).wait_recv()

        def block(n, carry):
            rows = pl.ds(pl.multiple_of(n * 256, 256), 256)
            u = cols[k].reshape(1024, 256)
            a = jnp.dot(p1t[0, rows, :], u, preferred_element_type=F32)
            b = jnp.dot(p1t[1, rows, :], u, preferred_element_type=F32)
            real = a[:, :128] - b[:, 128:]
            imag = a[:, 128:] + b[:, :128]
            four = pl.ds(n * 4, 4)
            ps[k, four, :, :128] = real.astype(BF16).reshape(4, 64, 128)
            ps[k, four, :, 128:] = imag.astype(BF16).reshape(4, 64, 128)
            return carry

        lax.fori_loop(0, 4, block, 0)

    def send_back(i, there):
        def send(n, carry):
            p = peer(n)
            pltpu.make_async_remote_copy(
                src_ref=ps.at[i, p],
                dst_ref=there.at[r],
                send_sem=send2.at[i],
                recv_sem=recv2.at[i],
                device_id=(partner, p),
                device_id_type=MESH,
            ).start()
            return carry

        lax.fori_loop(0, n_rad, send, 0)

    def second(i, carry):
        left(i)
        send_back(i, mv.at[i])
        return carry

    lax.fori_loop(0, kk - 1, second, 0)

    @pl.when(h == 0)
    def _():
        kin[0] = jnp.zeros_like(kin[0])

    @pl.when(h == n_hel - 1)
    def _():
        kin[kk + 1] = jnp.zeros_like(kin[kk + 1])

    def ends(low):
        return (1, kk + 1, 0) if low else (kk, 0, 1)

    def halo(low):
        own, there, n = ends(low)
        return pltpu.make_async_remote_copy(
            src_ref=kin.at[own],
            dst_ref=kin.at[there],
            send_sem=hsend.at[n],
            recv_sem=hrecv.at[n],
            device_id=(h - 1 if low else h + 1, r),
            device_id_type=MESH,
        )

    def quarter(low, q, target, by_helper):
        own, there, n = ends(low)
        rows = pl.ds(q * 512, 512)
        return pltpu.make_async_remote_copy(
            src_ref=kin.at[own, rows],
            dst_ref=relay if by_helper else kin.at[there, rows],
            send_sem=hsend.at[n],
            recv_sem=rrecv if by_helper else hrecv.at[n],
            device_id=(target, r),
            device_id_type=MESH,
        )

    def hand_on(low):
        own, there, n = ends(low)
        q = (h - middle - 1) // 2 if low else (h - 1) // 2
        rows = pl.ds(pl.multiple_of(q * 512, 512), 512)
        return pltpu.make_async_remote_copy(
            src_ref=relay,
            dst_ref=kin.at[there, rows],
            send_sem=rsend,
            recv_sem=hrecv.at[n],
            device_id=(middle - 1 if low else middle, r),
            device_id_type=MESH,
        )

    def arrived_at_helper(low):
        return quarter(low, 0, partner, True)

    def factors(k):
        g = h * kk + k
        row = lax.broadcasted_iota(jnp.int32, (8, 128), 0) % 4
        up, down = jnp.zeros((8, 128), F32), jnp.zeros((8, 128), F32)
        for j in range(4):
            to_up = jnp.where(g < n_hel * kk - 1, coup[j, g], 0.0)
            to_down = jnp.where(g > 0, coup[j, jnp.maximum(g - 1, 0)], 0.0)
            up = jnp.where(row == j, to_up, up)
            down = jnp.where(row == j, to_down, down)
        return up, down

    def at(slot, c, q):
        return tiles(kin[slot, chunk(q, c * 1024)])

    def finish(i):
        phase(mv.at[i], cosv, sinv, ph, 0, 64)
        propagate(ph, pbig, wide, 64)

        def store(q, carry):
            for c in range(2):
                kin[order(i) + 1, chunk(q, c * 1024)] = wide[c, chunk(q)].astype(BF16)
            return carry

        lax.fori_loop(0, 4, store, 0)

    def mix_early():
        k = 3 * z_lo
        up, down = factors(k)

        def block(q, carry):
            w = tiles(wr[chunk(q)])
            by = [w * (up * at(k + 2, c, q) + down * at(k, c, q)) for c in range(2)]
            rows = pl.ds(pl.multiple_of(q * 16, 16), 16)
            for c, x in enumerate((at(k + 1, 0, q) + by[1], at(k + 1, 1, q) - by[0])):
                early[c, rows] = flat(x).astype(BF16).reshape(16, 16, 128)
            return carry

        lax.fori_loop(0, 4, block, 0)

    low = 1 - z_lo

    def put_part(n, q, real, imag):
        part[n, 0, chunk(q)] = flat(real)
        part[n, 1, chunk(q)] = flat(imag)

    def part_first():
        up, down = factors(low)

        def block(q, carry):
            w = tiles(wr[chunk(q)])
            by = [w * (down * at(low, c, q)) for c in range(2)]
            put_part(0, q, at(low + 1, 0, q) + by[1], at(low + 1, 1, q) - by[0])
            wu[chunk(q)] = flat(w * up)
            return carry

        lax.fori_loop(0, 4, block, 0)

    def part_middle():
        up, down = factors(low + 1)

        def block(q, carry):
            w = tiles(wr[chunk(q)])
            by = [
                w * (up * at(low + 3, c, q) + down * at(low + 1, c, q))
                for c in range(2)
            ]
            put_part(1, q, by[1], -by[0])
            return carry

        lax.fori_loop(0, 4, block, 0)

    def part_last():
        up, down = factors(low + 2)

        def block(q, carry):
            w = tiles(wr[chunk(q)])
            by = [w * (up * at(low + 4, c, q)) for c in range(2)]
            put_part(2, q, at(low + 3, 0, q) + by[1], at(low + 3, 1, q) - by[0])
            wd[chunk(q)] = flat(w * down)
            return carry

        lax.fori_loop(0, 4, block, 0)

    def third(i):
        all_second(i).wait_recv()
        finish(i)

    def send_edge(low):
        @pl.when((h > 0) & (h != middle) if low else (h < n_hel - 1) & (h != middle - 1))
        def _():
            halo(low).start()

        @pl.when(is_high if low else is_low)
        def _():
            for q in range(4):
                if q == (0 if low else 3):
                    quarter(low, q, middle - 1 if low else middle, False).start()
                else:
                    helper = middle + 2 * q + 1 if low else 2 * q + 1
                    quarter(low, q, helper, True).start()

    third(0)

    @pl.when(z_lo == 1)
    def _():
        send_edge(True)

    @pl.when(z_lo == 0)
    def _():
        send_edge(False)

    @pl.when(carries_down)
    def _():
        arrived_at_helper(True).wait_recv()
        hand_on(True).start()

    @pl.when(carries_up)
    def _():
        arrived_at_helper(False).wait_recv()
        hand_on(False).start()

    left(kk - 1)
    for batch in range(2):
        half = pl.ds(batch * HALF, HALF)

        def send(n, carry):
            p = peer(n)
            pltpu.make_async_remote_copy(
                src_ref=ps.at[kk - 1, p, half],
                dst_ref=mvl.at[r, half],
                send_sem=send2.at[kk - 1 + batch],
                recv_sem=recv2.at[kk - 1 + batch],
                device_id=(partner, p),
                device_id_type=MESH,
            ).start()
            return carry

        lax.fori_loop(0, n_rad, send, 0)

    third(1)

    @pl.when(z_lo == 1)
    def _():
        send_edge(False)

    @pl.when(z_lo == 0)
    def _():
        send_edge(True)

    third(2)

    @pl.when((z_lo == 1) & (h < n_hel - 1))
    def _():
        halo(True).wait_recv()

    @pl.when((z_lo == 0) & (h > 0))
    def _():
        halo(False).wait_recv()

    mix_early()
    part_middle()

    @pl.when(z_lo == 1)
    def _():
        part_last()
        halo(False).wait_recv()
        part_first()

    @pl.when(z_lo == 0)
    def _():
        part_first()
        halo(True).wait_recv()
        part_last()

    all_last(0).wait_recv()
    phase(mvl, cosv, sinv, ph, 0, HALF)
    propagate(ph, pbig, wide, HALF)

    def first_rows(q, carry):
        combine(q, 0, wide, part, wu, wd, done)
        return carry

    lax.fori_loop(0, 2, first_rows, 0)
    all_last(1).wait_recv()

    def drain(i, carry):
        all_first(i).wait_send()
        return carry

    lax.fori_loop(0, kk, drain, 0)

    for i in range(kk - 1):
        all_second(i).wait_send()
    for batch in range(2):
        all_last(batch).wait_send()

    @pl.when(h > 0)
    def _():
        halo(True).wait_send()

    @pl.when(h < n_hel - 1)
    def _():
        halo(False).wait_send()

    @pl.when(carries_down)
    def _():
        hand_on(True).wait_send()

    @pl.when(carries_up)
    def _():
        hand_on(False).wait_send()


def solution(mesh):
    n_hel, n_rad = mesh.shape["hel"], mesh.shape["rad"]

    def per_device(packet, first, second, potential, coupling, weight):
        hbm = pl.BlockSpec(memory_space=pltpu.HBM)
        vmem = pl.BlockSpec(memory_space=pltpu.VMEM)
        dma = pltpu.SemaphoreType.DMA
        state = pl.pallas_call(
            functools.partial(kernel, n_hel, n_rad),
            out_shape=(
                pltpu.VMEM((2, 64, 16, 128), BF16),
                pltpu.VMEM((3, 2, HALF, 16, 128), BF16),
                pltpu.VMEM((1024, 1024), BF16),
                pltpu.VMEM((16, 64, 256), BF16),
                pltpu.VMEM((4, 4, 64, 128), F32),
                pltpu.VMEM((4, 4, 64, 128), F32),
                pltpu.VMEM((3, 2, 1024, 128), F32),
                pltpu.VMEM((1024, 128), F32),
                pltpu.VMEM((1024, 128), F32),
            ),
            in_specs=[hbm] * 6,
            out_specs=[vmem] * 9,
            scratch_shapes=[
                pltpu.VMEM((4, 2, 64, 4, 512), BF16),
                pltpu.VMEM((2, 512, 512), BF16),
                pltpu.VMEM((2, 1024, 1024), BF16),
                pltpu.VMEM((2, 1024, 1024), BF16),
                pltpu.VMEM((64, 4, 512), F32),
                pltpu.VMEM((64, 512), F32),
                pltpu.VMEM((1024, 128), F32),
                pltpu.SMEM((4, 64), F32),
                pltpu.VMEM((8, 256, 128), F32),
                pltpu.VMEM((2, 1024, 128), F32),
                pltpu.VMEM((4, 16, 64, 256), BF16),
                pltpu.VMEM((4, 16, 64, 256), BF16),
                pltpu.VMEM((4, 16, 64, 256), BF16),
                pltpu.VMEM((3, 16, 64, 256), BF16),
                pltpu.VMEM((256, 1024), BF16),
                pltpu.VMEM((6, 2048, 128), BF16),
                pltpu.VMEM((512, 128), BF16),
                dma((5,)),
                dma((4, 2)),
                dma((4,)),
                dma((4,)),
                dma((5,)),
                dma((5,)),
                dma((2,)),
                dma((2,)),
                dma,
                dma,
            ],
            compiler_params=pltpu.CompilerParams(
                collective_id=0,
                has_side_effects=True,
                vmem_limit_bytes=48 * 2**20,
            ),
        )(
            *(
                pltpu.with_memory_space_constraint(a, pltpu.HBM)
                for a in (coupling.T, packet, first, second, potential, weight)
            )
        )
        rows = pl.pallas_call(
            functools.partial(last_rows, n_hel),
            out_shape=pltpu.HBM((64, 2, 4, 16, 128), BF16),
            in_specs=[vmem] * 9,
            out_specs=hbm,
            scratch_shapes=[
                pltpu.VMEM((4 * HALF, 1024), BF16),
                pltpu.VMEM((2, HALF * 16, 128), F32),
                pltpu.VMEM((3, 2, HALF, 16, 128), BF16),
                dma((20,)),
            ],
            compiler_params=pltpu.CompilerParams(vmem_limit_bytes=16 * 2**20),
        )(*(pltpu.with_memory_space_constraint(a, pltpu.VMEM) for a in state))
        rows = rows.reshape(64, 2, 4, 4, 4, 128)
        return rows.transpose(0, 1, 2, 4, 3, 5).reshape(packet.shape)

    return jax.shard_map(
        per_device,
        mesh=mesh,
        in_specs=(
            P("rad", None, "hel", None, None),
            P(),
            P(),
            P("rad", None, None),
            P(),
            P("rad", None),
        ),
        out_specs=P("rad", None, "hel", None, None),
        check_vma=False,
    )
```

```python
import functools

import jax
import jax.numpy as jnp
from jax import lax
from jax.experimental import pallas as pl
from jax.experimental.pallas import tpu as pltpu
from jax.sharding import PartitionSpec as P

MESH = pl.DeviceIdType.MESH
BF16 = jnp.bfloat16
F32 = jnp.float32
BATCHES = ((0, 32), (32, 32))
MOST, REST = BATCHES[-1]


def place_of(j, s):
    return j * 4 + (s - j) % 4


def phase(moved, cosv, sinv, ph, base, count):
    here = slice(base, base + count)
    for j in range(4):
        rows = slice(j * count, (j + 1) * count)
        for s in range(4):
            p = place_of(j, s)
            re, im = moved[p, here, :128].astype(F32), moved[p, here, 128:].astype(F32)
            c, sn = cosv[j, s, here], sinv[j, s, here]
            ph[rows, s * 128 : (s + 1) * 128] = (re * c + im * sn).astype(BF16)
            ph[rows, 512 + s * 128 : 512 + (s + 1) * 128] = (im * c - re * sn).astype(
                BF16
            )


def propagate(ph, pbig, wide, count):
    for s in range(4):
        y = jnp.dot(
            ph[: 4 * count],
            pbig[:, s * 256 : (s + 1) * 256],
            preferred_element_type=F32,
        )
        for c in range(2):
            for j in range(4):
                wide.at[c][pl.ds(s * 4 + j, count, stride=16), :] = y[
                    j * count : (j + 1) * count, c * 128 : (c + 1) * 128
                ]


def combine(q, base, first, low, wide, part, wu, wd, res):
    new, rows = chunk(q), chunk(q, base * 16)
    re = wide[0, new].astype(BF16).astype(F32)
    im = wide[1, new].astype(BF16).astype(F32)
    up, down = wu[rows], wd[rows]
    values = (
        (part[0, 0, rows] + up * im, part[0, 1, rows] - up * re),
        (part[1, 0, rows] + re, part[1, 1, rows] + im),
        (part[2, 0, rows] + down * im, part[2, 1, rows] - down * re),
    )
    for n in range(3):
        for c in range(2):
            res[pl.ds(first + q * 16, 16), c, low + n] = (
                values[n][c].astype(BF16).reshape(16, 16, 128)
            )


def tiles(x):
    return x.astype(F32).reshape(32, 8, 128)


def flat(x):
    return x.reshape(256, 128)


def chunk(q, base=0):
    return pl.ds(pl.multiple_of(base + q * 256, 256), 256)


def last_rows(
    n_hel,
    done,
    pbig,
    moved,
    cosv,
    sinv,
    part,
    wu,
    wd,
    out,
    ph,
    wide,
    res,
    sems,
):
    z_lo = lax.axis_index("hel") // (n_hel // 2)
    low = 1 - z_lo

    copies = [
        pltpu.make_async_copy(
            done.at[pl.ds(n * 16, 16)], out.at[pl.ds(n * 16, 16)], sems.at[n]
        )
        for n in range(MOST // 16)
    ]
    for copy in copies:
        copy.start()
    phase(moved, cosv, sinv, ph, MOST, REST)
    for c in range(2):
        res[:, c, 3 * z_lo] = done[MOST:, c, 3 * z_lo]
    propagate(ph, pbig, wide, REST)
    for q in range(REST // 16):
        combine(q, MOST, 0, low, wide, part, wu, wd, res)
    last = pltpu.make_async_copy(res, out.at[pl.ds(MOST, REST)], sems.at[3])
    last.start()
    for copy in copies:
        copy.wait()
    last.wait()


def kernel(
    n_hel,
    n_rad,
    coup_hbm,
    pk,
    p1,
    p2,
    pot,
    rw,
    done,
    pbig,
    mvl,
    cosv,
    sinv,
    part,
    wu,
    wd,
    pkv,
    p2v,
    p1v,
    p1t,
    potv,
    wv,
    wr,
    coup,
    fscr,
    wide,
    hs,
    cols,
    ps,
    mv,
    ph,
    kin,
    relay,
    load_sem,
    pk_sem,
    send1,
    recv1,
    send2,
    recv2,
    hsend,
    hrecv,
    rsend,
    rrecv,
):
    kk = pkv.shape[0]
    h = lax.axis_index("hel")
    r = lax.axis_index("rad")
    middle = n_hel // 2
    partner = lax.rem(h + middle, n_hel)
    zh, y = r // 4, lax.rem(r, 4)
    z_lo = h // middle

    def order(i):
        return jnp.where(z_lo == 0, lax.rem(3 + i, 4), lax.rem(3 * i, 4))

    def peer(i):
        b = i // 4
        dy = jnp.where(b == 0, 2, jnp.where(b == 3, 0, 2 * b - 1))
        return lax.rem(zh + lax.rem(i, 4) + 1 + z_lo, 4) * 4 + lax.rem(y + dy, 4)

    is_low, is_high = h == middle - 1, h == middle
    carries_down = (h > middle + 1) & (lax.rem(h, 2) == 1)
    carries_up = (h < middle - 2) & (lax.rem(h, 2) == 1)

    barrier = pltpu.get_barrier_semaphore()

    def greet_one(target, rad):
        pl.semaphore_signal(
            barrier, inc=1, device_id=(target, rad), device_id_type=MESH
        )

    def greet(i, carry):
        greet_one(partner, peer(i))
        return carry

    lax.fori_loop(0, n_rad, greet, 0)

    @pl.when(h > 0)
    def _():
        greet_one(h - 1, r)

    @pl.when(h < n_hel - 1)
    def _():
        greet_one(h + 1, r)

    @pl.when(carries_down)
    def _():
        greet_one(middle, r)

    @pl.when(carries_up)
    def _():
        greet_one(middle - 1, r)

    @pl.when(is_low)
    def _():
        for q in range(1, 4):
            greet_one(middle + 2 * q + 1, r)

    @pl.when(is_high)
    def _():
        for q in range(3):
            greet_one(2 * q + 1, r)

    greeted = n_rad + jnp.where(h > 0, 1, 0) + jnp.where(h < n_hel - 1, 1, 0)
    greeted += jnp.where(is_low | is_high, 3, 0)
    greeted += jnp.where(carries_down | carries_up, 1, 0)

    def load_packet(i):
        k = order(i)
        return [
            pltpu.make_async_copy(pk.at[:, c, k], pkv.at[k, c], pk_sem.at[i, c])
            for c in range(2)
        ]

    load_p2 = pltpu.make_async_copy(p2, p2v, load_sem.at[0])
    load_p1 = pltpu.make_async_copy(p1, p1v, load_sem.at[1])
    load_pot = pltpu.make_async_copy(pot, potv, load_sem.at[2])
    load_w = pltpu.make_async_copy(rw, wv, load_sem.at[3])
    load_coup = pltpu.make_async_copy(coup_hbm, coup, load_sem.at[4])
    load_p2.start()
    for i in range(kk):
        for copy in load_packet(i):
            copy.start()
    load_p1.start()
    load_pot.start()
    load_w.start()
    load_coup.start()

    load_p2.wait()

    def first(i, carry):
        k = order(i)
        for copy in load_packet(i):
            copy.wait()
        x = [pkv[k, c].reshape(256, 512) for c in range(2)]
        for t in range(2):
            lanes = slice(t * 256, (t + 1) * 256)

            def product(c, d):
                return jnp.dot(x[c], p2v[d, :, lanes], preferred_element_type=F32)

            real = product(0, 0) - product(1, 1)
            imag = product(0, 1) + product(1, 0)
            for s in range(2):
                fscr[4 * t + 2 * s] = real[:, s * 128 : (s + 1) * 128]
                fscr[4 * t + 2 * s + 1] = imag[:, s * 128 : (s + 1) * 128]
            for j in range(4):
                for s in (2 * t, 2 * t + 1):
                    for c in range(2):
                        rows = fscr.at[2 * s + c][pl.ds(j, 64, stride=4), :]
                        hs[i, place_of(j, s), :, c * 128 : (c + 1) * 128] = rows.astype(
                            BF16
                        )

        @pl.when(i == 0)
        def _():
            pl.semaphore_wait(barrier, greeted)

        def send(n, carry):
            p = peer(n)
            pltpu.make_async_remote_copy(
                src_ref=hs.at[i, p],
                dst_ref=cols.at[i, r],
                send_sem=send1.at[i],
                recv_sem=recv1.at[i],
                device_id=(partner, p),
                device_id_type=MESH,
            ).start()
            return carry

        lax.fori_loop(0, n_rad, send, 0)
        return carry

    lax.fori_loop(0, kk, first, 0)

    for s in range(4):
        lanes = slice(s * 128, (s + 1) * 128)
        real, imag = p2v[0, :, lanes], p2v[1, :, lanes]
        pbig[:512, s * 256 : s * 256 + 128] = real
        pbig[:512, s * 256 + 128 : (s + 1) * 256] = imag
        pbig[512:, s * 256 : s * 256 + 128] = -imag
        pbig[512:, s * 256 + 128 : (s + 1) * 256] = real

    load_p1.wait()

    def flip(n, carry):
        rows = pl.ds(pl.multiple_of(n * 128, 128), 128)
        for c in range(2):
            p1t[c, rows, :] = p1v[c, :, rows].T
        return carry

    lax.fori_loop(0, 8, flip, 0)
    load_pot.wait()
    for s in range(4):
        fscr[s] = potv[:, :, s * 128 : (s + 1) * 128].reshape(256, 128)

    def phases(s, carry):
        for j in range(4):
            angle = fscr.at[s][pl.ds(j, 64, stride=4), :]
            cosv[j, s] = jnp.cos(angle)
            sinv[j, s] = jnp.sin(angle)
        return carry

    lax.fori_loop(0, 4, phases, 0)
    load_w.wait()
    load_coup.wait()
    for s in range(4):
        for j in range(4):
            wr[pl.ds(s * 4 + j, 64, stride=16), :] = wv[:, s * 128 : (s + 1) * 128]

    def whole(src, dst, send_sem, recv_sem):
        return pltpu.make_async_remote_copy(
            src_ref=src,
            dst_ref=dst,
            send_sem=send_sem,
            recv_sem=recv_sem,
            device_id=(partner, r),
            device_id_type=MESH,
        )

    def all_first(k):
        return whole(hs.at[k], cols.at[k], send1.at[k], recv1.at[k])

    def all_second(i):
        return whole(ps.at[i], mv.at[i], send2.at[i], recv2.at[i])

    def all_last(n):
        part = pl.ds(*BATCHES[n])
        return whole(
            ps.at[3, :, part], mvl.at[:, part], send2.at[3 + n], recv2.at[3 + n]
        )

    def left(k):
        all_first(k).wait_recv()

        def block(n, carry):
            rows = pl.ds(pl.multiple_of(n * 256, 256), 256)
            u = cols[k].reshape(1024, 256)
            a = jnp.dot(p1t[0, rows, :], u, preferred_element_type=F32)
            b = jnp.dot(p1t[1, rows, :], u, preferred_element_type=F32)
            real = a[:, :128] - b[:, 128:]
            imag = a[:, 128:] + b[:, :128]
            four = pl.ds(n * 4, 4)
            ps[k, four, :, :128] = real.astype(BF16).reshape(4, 64, 128)
            ps[k, four, :, 128:] = imag.astype(BF16).reshape(4, 64, 128)
            return carry

        lax.fori_loop(0, 4, block, 0)

    def send_back(i, there):
        def send(n, carry):
            p = peer(n)
            pltpu.make_async_remote_copy(
                src_ref=ps.at[i, p],
                dst_ref=there.at[r],
                send_sem=send2.at[i],
                recv_sem=recv2.at[i],
                device_id=(partner, p),
                device_id_type=MESH,
            ).start()
            return carry

        lax.fori_loop(0, n_rad, send, 0)

    def second(i, carry):
        left(i)
        send_back(i, mv.at[i])
        return carry

    lax.fori_loop(0, kk - 1, second, 0)

    @pl.when(h == 0)
    def _():
        kin[0] = jnp.zeros_like(kin[0])

    @pl.when(h == n_hel - 1)
    def _():
        kin[kk + 1] = jnp.zeros_like(kin[kk + 1])

    def ends(low):
        return (1, kk + 1, 0) if low else (kk, 0, 1)

    def halo(low):
        own, there, n = ends(low)
        return pltpu.make_async_remote_copy(
            src_ref=kin.at[own],
            dst_ref=kin.at[there],
            send_sem=hsend.at[n],
            recv_sem=hrecv.at[n],
            device_id=(h - 1 if low else h + 1, r),
            device_id_type=MESH,
        )

    def quarter(low, q, target, by_helper):
        own, there, n = ends(low)
        rows = pl.ds(q * 512, 512)
        return pltpu.make_async_remote_copy(
            src_ref=kin.at[own, rows],
            dst_ref=relay if by_helper else kin.at[there, rows],
            send_sem=hsend.at[n],
            recv_sem=rrecv if by_helper else hrecv.at[n],
            device_id=(target, r),
            device_id_type=MESH,
        )

    def hand_on(low):
        own, there, n = ends(low)
        q = (h - middle - 1) // 2 if low else (h - 1) // 2
        rows = pl.ds(pl.multiple_of(q * 512, 512), 512)
        return pltpu.make_async_remote_copy(
            src_ref=relay,
            dst_ref=kin.at[there, rows],
            send_sem=rsend,
            recv_sem=hrecv.at[n],
            device_id=(middle - 1 if low else middle, r),
            device_id_type=MESH,
        )

    def arrived_at_helper(low):
        return quarter(low, 0, partner, True)

    def factors(k):
        g = h * kk + k
        row = lax.broadcasted_iota(jnp.int32, (8, 128), 0) % 4
        up, down = jnp.zeros((8, 128), F32), jnp.zeros((8, 128), F32)
        for j in range(4):
            to_up = jnp.where(g < n_hel * kk - 1, coup[j, g], 0.0)
            to_down = jnp.where(g > 0, coup[j, jnp.maximum(g - 1, 0)], 0.0)
            up = jnp.where(row == j, to_up, up)
            down = jnp.where(row == j, to_down, down)
        return up, down

    def at(slot, c, q):
        return tiles(kin[slot, chunk(q, c * 1024)])

    def finish(i):
        phase(mv.at[i], cosv, sinv, ph, 0, 64)
        propagate(ph, pbig, wide, 64)

        def store(q, carry):
            for c in range(2):
                kin[order(i) + 1, chunk(q, c * 1024)] = wide[c, chunk(q)].astype(BF16)
            return carry

        lax.fori_loop(0, 4, store, 0)

    def mix_early():
        k = 3 * z_lo
        up, down = factors(k)

        def block(q, carry):
            w = tiles(wr[chunk(q)])
            by = [w * (up * at(k + 2, c, q) + down * at(k, c, q)) for c in range(2)]
            rows = pl.ds(pl.multiple_of(q * 16, 16), 16)
            for c, x in enumerate((at(k + 1, 0, q) + by[1], at(k + 1, 1, q) - by[0])):
                done[rows, c, k] = flat(x).astype(BF16).reshape(16, 16, 128)
            return carry

        lax.fori_loop(0, 4, block, 0)

    low = 1 - z_lo

    def put_part(n, q, real, imag):
        part[n, 0, chunk(q)] = flat(real)
        part[n, 1, chunk(q)] = flat(imag)

    def part_first():
        up, down = factors(low)

        def block(q, carry):
            w = tiles(wr[chunk(q)])
            by = [w * (down * at(low, c, q)) for c in range(2)]
            put_part(0, q, at(low + 1, 0, q) + by[1], at(low + 1, 1, q) - by[0])
            wu[chunk(q)] = flat(w * up)
            return carry

        lax.fori_loop(0, 4, block, 0)

    def part_middle():
        up, down = factors(low + 1)

        def block(q, carry):
            w = tiles(wr[chunk(q)])
            by = [
                w * (up * at(low + 3, c, q) + down * at(low + 1, c, q))
                for c in range(2)
            ]
            put_part(1, q, by[1], -by[0])
            return carry

        lax.fori_loop(0, 4, block, 0)

    def part_last():
        up, down = factors(low + 2)

        def block(q, carry):
            w = tiles(wr[chunk(q)])
            by = [w * (up * at(low + 4, c, q)) for c in range(2)]
            put_part(2, q, at(low + 3, 0, q) + by[1], at(low + 3, 1, q) - by[0])
            wd[chunk(q)] = flat(w * down)
            return carry

        lax.fori_loop(0, 4, block, 0)

    def third(i):
        all_second(i).wait_recv()
        finish(i)

    def send_edge(low):
        @pl.when((h > 0) & (h != middle) if low else (h < n_hel - 1) & (h != middle - 1))
        def _():
            halo(low).start()

        @pl.when(is_high if low else is_low)
        def _():
            for q in range(4):
                if q == (0 if low else 3):
                    quarter(low, q, middle - 1 if low else middle, False).start()
                else:
                    helper = middle + 2 * q + 1 if low else 2 * q + 1
                    quarter(low, q, helper, True).start()

    third(0)

    @pl.when(z_lo == 1)
    def _():
        send_edge(True)

    @pl.when(z_lo == 0)
    def _():
        send_edge(False)

    @pl.when(carries_down)
    def _():
        arrived_at_helper(True).wait_recv()
        hand_on(True).start()

    @pl.when(carries_up)
    def _():
        arrived_at_helper(False).wait_recv()
        hand_on(False).start()

    left(kk - 1)
    for batch, points in enumerate(BATCHES):
        here = pl.ds(*points)

        def send(n, carry):
            p = peer(n)
            pltpu.make_async_remote_copy(
                src_ref=ps.at[kk - 1, p, here],
                dst_ref=mvl.at[r, here],
                send_sem=send2.at[kk - 1 + batch],
                recv_sem=recv2.at[kk - 1 + batch],
                device_id=(partner, p),
                device_id_type=MESH,
            ).start()
            return carry

        lax.fori_loop(0, n_rad, send, 0)

    third(1)

    @pl.when(z_lo == 1)
    def _():
        send_edge(False)

    @pl.when(z_lo == 0)
    def _():
        send_edge(True)

    third(2)

    @pl.when((z_lo == 1) & (h < n_hel - 1))
    def _():
        halo(True).wait_recv()

    @pl.when((z_lo == 0) & (h > 0))
    def _():
        halo(False).wait_recv()

    mix_early()
    part_middle()

    @pl.when(z_lo == 1)
    def _():
        part_last()
        halo(False).wait_recv()
        part_first()

    @pl.when(z_lo == 0)
    def _():
        part_first()
        halo(True).wait_recv()
        part_last()

    for batch, (base, count) in enumerate(BATCHES[:-1]):
        all_last(batch).wait_recv()
        phase(mvl, cosv, sinv, ph, base, count)
        propagate(ph, pbig, wide, count)
        for q in range(count // 16):
            combine(q, base, base, low, wide, part, wu, wd, done)
    all_last(len(BATCHES) - 1).wait_recv()

    def drain(i, carry):
        all_first(i).wait_send()
        return carry

    lax.fori_loop(0, kk, drain, 0)

    for i in range(kk - 1):
        all_second(i).wait_send()
    for batch in range(len(BATCHES)):
        all_last(batch).wait_send()

    @pl.when(h > 0)
    def _():
        halo(True).wait_send()

    @pl.when(h < n_hel - 1)
    def _():
        halo(False).wait_send()

    @pl.when(carries_down)
    def _():
        hand_on(True).wait_send()

    @pl.when(carries_up)
    def _():
        hand_on(False).wait_send()


def solution(mesh):
    n_hel, n_rad = mesh.shape["hel"], mesh.shape["rad"]

    def per_device(packet, first, second, potential, coupling, weight):
        hbm = pl.BlockSpec(memory_space=pltpu.HBM)
        vmem = pl.BlockSpec(memory_space=pltpu.VMEM)
        dma = pltpu.SemaphoreType.DMA
        state = pl.pallas_call(
            functools.partial(kernel, n_hel, n_rad),
            out_shape=(
                pltpu.VMEM((64, 2, 4, 16, 128), BF16),
                pltpu.VMEM((1024, 1024), BF16),
                pltpu.VMEM((16, 64, 256), BF16),
                pltpu.VMEM((4, 4, 64, 128), F32),
                pltpu.VMEM((4, 4, 64, 128), F32),
                pltpu.VMEM((3, 2, 1024, 128), F32),
                pltpu.VMEM((1024, 128), F32),
                pltpu.VMEM((1024, 128), F32),
            ),
            in_specs=[hbm] * 6,
            out_specs=[vmem] * 8,
            scratch_shapes=[
                pltpu.VMEM((4, 2, 64, 4, 512), BF16),
                pltpu.VMEM((2, 512, 512), BF16),
                pltpu.VMEM((2, 1024, 1024), BF16),
                pltpu.VMEM((2, 1024, 1024), BF16),
                pltpu.VMEM((64, 4, 512), F32),
                pltpu.VMEM((64, 512), F32),
                pltpu.VMEM((1024, 128), F32),
                pltpu.SMEM((4, 64), F32),
                pltpu.VMEM((8, 256, 128), F32),
                pltpu.VMEM((2, 1024, 128), F32),
                pltpu.VMEM((4, 16, 64, 256), BF16),
                pltpu.VMEM((4, 16, 64, 256), BF16),
                pltpu.VMEM((4, 16, 64, 256), BF16),
                pltpu.VMEM((3, 16, 64, 256), BF16),
                pltpu.VMEM((256, 1024), BF16),
                pltpu.VMEM((6, 2048, 128), BF16),
                pltpu.VMEM((512, 128), BF16),
                dma((5,)),
                dma((4, 2)),
                dma((4,)),
                dma((4,)),
                dma((5,)),
                dma((5,)),
                dma((2,)),
                dma((2,)),
                dma,
                dma,
            ],
            compiler_params=pltpu.CompilerParams(
                collective_id=0,
                has_side_effects=True,
                vmem_limit_bytes=48 * 2**20,
            ),
        )(
            *(
                pltpu.with_memory_space_constraint(a, pltpu.HBM)
                for a in (coupling.T, packet, first, second, potential, weight)
            )
        )
        rows = pl.pallas_call(
            functools.partial(last_rows, n_hel),
            out_shape=pltpu.HBM((64, 2, 4, 16, 128), BF16),
            in_specs=[vmem] * 8,
            out_specs=hbm,
            scratch_shapes=[
                pltpu.VMEM((4 * REST, 1024), BF16),
                pltpu.VMEM((2, REST * 16, 128), F32),
                pltpu.VMEM((REST, 2, 4, 16, 128), BF16),
                dma((4,)),
            ],
            compiler_params=pltpu.CompilerParams(vmem_limit_bytes=16 * 2**20),
        )(*(pltpu.with_memory_space_constraint(a, pltpu.VMEM) for a in state))
        rows = rows.reshape(64, 2, 4, 4, 4, 128)
        return rows.transpose(0, 1, 2, 4, 3, 5).reshape(packet.shape)

    return jax.shard_map(
        per_device,
        mesh=mesh,
        in_specs=(
            P("rad", None, "hel", None, None),
            P(),
            P(),
            P("rad", None, None),
            P(),
            P("rad", None),
        ),
        out_specs=P("rad", None, "hel", None, None),
        check_vma=False,
    )
```

```python
import functools

import jax
import jax.numpy as jnp
from jax import lax
from jax.experimental import pallas as pl
from jax.experimental.pallas import tpu as pltpu
from jax.sharding import PartitionSpec as P

MESH = pl.DeviceIdType.MESH
BF16 = jnp.bfloat16
F32 = jnp.float32
BATCHES = ((0, 32), (32, 32))
MOST, REST = BATCHES[-1]


def place_of(j, s):
    return j * 4 + (s - j) % 4


def phase(moved, cosv, sinv, ph, base, count):
    here = slice(base, base + count)
    for j in range(4):
        rows = slice(j * count, (j + 1) * count)
        for s in range(4):
            p = place_of(j, s)
            re, im = moved[p, here, :128].astype(F32), moved[p, here, 128:].astype(F32)
            c, sn = cosv[j, s, here], sinv[j, s, here]
            ph[rows, s * 128 : (s + 1) * 128] = (re * c + im * sn).astype(BF16)
            ph[rows, 512 + s * 128 : 512 + (s + 1) * 128] = (im * c - re * sn).astype(
                BF16
            )


def propagate(ph, pbig, wide, count):
    for s in range(4):
        y = jnp.dot(
            ph[: 4 * count],
            pbig[:, s * 256 : (s + 1) * 256],
            preferred_element_type=F32,
        )
        for c in range(2):
            for j in range(4):
                wide.at[c][pl.ds(s * 4 + j, count, stride=16), :] = y[
                    j * count : (j + 1) * count, c * 128 : (c + 1) * 128
                ]


def combine(q, base, first, low, wide, part, wu, wd, res):
    new, rows = chunk(q), chunk(q, base * 16)
    re = wide[0, new].astype(BF16).astype(F32)
    im = wide[1, new].astype(BF16).astype(F32)
    up, down = wu[rows], wd[rows]
    values = (
        (part[0, 0, rows] + up * im, part[0, 1, rows] - up * re),
        (part[1, 0, rows] + re, part[1, 1, rows] + im),
        (part[2, 0, rows] + down * im, part[2, 1, rows] - down * re),
    )
    for n in range(3):
        for c in range(2):
            res[pl.ds(first + q * 16, 16), c, low + n] = (
                values[n][c].astype(BF16).reshape(16, 16, 128)
            )


def tiles(x):
    return x.astype(F32).reshape(32, 8, 128)


def flat(x):
    return x.reshape(256, 128)


def chunk(q, base=0):
    return pl.ds(pl.multiple_of(base + q * 256, 256), 256)


def last_rows(
    n_hel,
    done,
    pbig,
    moved,
    cosv,
    sinv,
    part,
    wu,
    wd,
    out,
    ph,
    wide,
    res,
    sems,
):
    z_lo = lax.axis_index("hel") // (n_hel // 2)
    low = 1 - z_lo

    copies = [
        pltpu.make_async_copy(
            done.at[pl.ds(n * 16, 16)], out.at[pl.ds(n * 16, 16)], sems.at[n]
        )
        for n in range(MOST // 16)
    ]
    for copy in copies:
        copy.start()
    phase(moved, cosv, sinv, ph, MOST, REST)
    for c in range(2):
        res[:, c, 3 * z_lo] = done[MOST:, c, 3 * z_lo]
    propagate(ph, pbig, wide, REST)
    for q in range(REST // 16):
        combine(q, MOST, 0, low, wide, part, wu, wd, res)
    last = pltpu.make_async_copy(res, out.at[pl.ds(MOST, REST)], sems.at[3])
    last.start()
    for copy in copies:
        copy.wait()
    last.wait()


def kernel(
    n_hel,
    n_rad,
    coup_hbm,
    pk,
    p1,
    p2,
    pot,
    rw,
    done,
    pbig,
    mvl,
    cosv,
    sinv,
    part,
    wu,
    wd,
    pkv,
    p2v,
    p1v,
    p1t,
    potv,
    wv,
    wr,
    coup,
    fscr,
    wide,
    hs,
    cols,
    ps,
    mv,
    ph,
    kin,
    relay,
    load_sem,
    pk_sem,
    send1,
    recv1,
    send2,
    recv2,
    hsend,
    hrecv,
    rsend,
    rrecv,
):
    kk = pkv.shape[0]
    h = lax.axis_index("hel")
    r = lax.axis_index("rad")
    middle = n_hel // 2
    partner = lax.rem(h + middle, n_hel)
    zh, y = r // 4, lax.rem(r, 4)
    z_lo = h // middle

    def order(i):
        return jnp.where(z_lo == 0, lax.rem(3 + i, 4), lax.rem(3 * i, 4))

    def peer(i):
        b = i // 4
        dy = jnp.where(b == 0, 2, jnp.where(b == 3, 0, 2 * b - 1))
        return lax.rem(zh + lax.rem(i, 4) + 1 + z_lo, 4) * 4 + lax.rem(y + dy, 4)

    is_low, is_high = h == middle - 1, h == middle
    carries_down = (h > middle + 1) & (lax.rem(h, 2) == 1)
    carries_up = (h < middle - 2) & (lax.rem(h, 2) == 1)

    barrier = pltpu.get_barrier_semaphore()

    def greet_one(target, rad):
        pl.semaphore_signal(
            barrier, inc=1, device_id=(target, rad), device_id_type=MESH
        )

    def greet(i, carry):
        greet_one(partner, peer(i))
        return carry

    lax.fori_loop(0, n_rad, greet, 0)

    @pl.when(h > 0)
    def _():
        greet_one(h - 1, r)

    @pl.when(h < n_hel - 1)
    def _():
        greet_one(h + 1, r)

    @pl.when(carries_down)
    def _():
        greet_one(middle, r)

    @pl.when(carries_up)
    def _():
        greet_one(middle - 1, r)

    @pl.when(is_low)
    def _():
        for q in range(1, 4):
            greet_one(middle + 2 * q + 1, r)

    @pl.when(is_high)
    def _():
        for q in range(3):
            greet_one(2 * q + 1, r)

    greeted = n_rad + jnp.where(h > 0, 1, 0) + jnp.where(h < n_hel - 1, 1, 0)
    greeted += jnp.where(is_low | is_high, 3, 0)
    greeted += jnp.where(carries_down | carries_up, 1, 0)

    def load_packet(i):
        k = order(i)
        return [
            pltpu.make_async_copy(pk.at[:, c, k], pkv.at[k, c], pk_sem.at[i, c])
            for c in range(2)
        ]

    load_p2 = pltpu.make_async_copy(p2, p2v, load_sem.at[0])
    load_p1 = pltpu.make_async_copy(p1, p1v, load_sem.at[1])
    load_pot = pltpu.make_async_copy(pot, potv, load_sem.at[2])
    load_w = pltpu.make_async_copy(rw, wv, load_sem.at[3])
    load_coup = pltpu.make_async_copy(coup_hbm, coup, load_sem.at[4])
    load_p2.start()
    for i in range(kk):
        for copy in load_packet(i):
            copy.start()
    load_p1.start()
    load_pot.start()
    load_w.start()
    load_coup.start()

    load_p2.wait()

    def first(i, carry):
        k = order(i)
        for copy in load_packet(i):
            copy.wait()
        x = [pkv[k, c].reshape(256, 512) for c in range(2)]
        for t in range(2):
            lanes = slice(t * 256, (t + 1) * 256)

            def product(c, d):
                return jnp.dot(x[c], p2v[d, :, lanes], preferred_element_type=F32)

            real = product(0, 0) - product(1, 1)
            imag = product(0, 1) + product(1, 0)
            for s in range(2):
                fscr[4 * t + 2 * s] = real[:, s * 128 : (s + 1) * 128]
                fscr[4 * t + 2 * s + 1] = imag[:, s * 128 : (s + 1) * 128]
            for j in range(4):
                for s in (2 * t, 2 * t + 1):
                    for c in range(2):
                        rows = fscr.at[2 * s + c][pl.ds(j, 64, stride=4), :]
                        hs[i, place_of(j, s), :, c * 128 : (c + 1) * 128] = rows.astype(
                            BF16
                        )

        @pl.when(i == 0)
        def _():
            pl.semaphore_wait(barrier, greeted)

        def send(n, carry):
            p = peer(n)
            pltpu.make_async_remote_copy(
                src_ref=hs.at[i, p],
                dst_ref=cols.at[i, r],
                send_sem=send1.at[i],
                recv_sem=recv1.at[i],
                device_id=(partner, p),
                device_id_type=MESH,
            ).start()
            return carry

        lax.fori_loop(0, n_rad, send, 0)
        return carry

    lax.fori_loop(0, kk, first, 0)

    for s in range(4):
        lanes = slice(s * 128, (s + 1) * 128)
        real, imag = p2v[0, :, lanes], p2v[1, :, lanes]
        pbig[:512, s * 256 : s * 256 + 128] = real
        pbig[:512, s * 256 + 128 : (s + 1) * 256] = imag
        pbig[512:, s * 256 : s * 256 + 128] = -imag
        pbig[512:, s * 256 + 128 : (s + 1) * 256] = real

    load_p1.wait()

    def flip(n, carry):
        rows = pl.ds(pl.multiple_of(n * 128, 128), 128)
        for c in range(2):
            p1t[c, rows, :] = p1v[c, :, rows].T
        return carry

    lax.fori_loop(0, 8, flip, 0)
    load_pot.wait()
    for s in range(4):
        fscr[s] = potv[:, :, s * 128 : (s + 1) * 128].reshape(256, 128)

    def phases(s, carry):
        for j in range(4):
            angle = fscr.at[s][pl.ds(j, 64, stride=4), :]
            cosv[j, s] = jnp.cos(angle)
            sinv[j, s] = jnp.sin(angle)
        return carry

    lax.fori_loop(0, 4, phases, 0)
    load_w.wait()
    load_coup.wait()
    for s in range(4):
        for j in range(4):
            wr[pl.ds(s * 4 + j, 64, stride=16), :] = wv[:, s * 128 : (s + 1) * 128]

    def whole(src, dst, send_sem, recv_sem):
        return pltpu.make_async_remote_copy(
            src_ref=src,
            dst_ref=dst,
            send_sem=send_sem,
            recv_sem=recv_sem,
            device_id=(partner, r),
            device_id_type=MESH,
        )

    def all_first(k):
        return whole(hs.at[k], cols.at[k], send1.at[k], recv1.at[k])

    def all_second(i):
        return whole(ps.at[i], mv.at[i], send2.at[i], recv2.at[i])

    def all_last(n):
        part = pl.ds(*BATCHES[n])
        return whole(
            ps.at[3, :, part], mvl.at[:, part], send2.at[3 + n], recv2.at[3 + n]
        )

    def left(k):
        all_first(k).wait_recv()

        def block(n, carry):
            rows = pl.ds(pl.multiple_of(n * 256, 256), 256)
            u = cols[k].reshape(1024, 256)
            a = jnp.dot(p1t[0, rows, :], u, preferred_element_type=F32)
            b = jnp.dot(p1t[1, rows, :], u, preferred_element_type=F32)
            real = a[:, :128] - b[:, 128:]
            imag = a[:, 128:] + b[:, :128]
            four = pl.ds(n * 4, 4)
            ps[k, four, :, :128] = real.astype(BF16).reshape(4, 64, 128)
            ps[k, four, :, 128:] = imag.astype(BF16).reshape(4, 64, 128)
            return carry

        lax.fori_loop(0, 4, block, 0)

    def send_back(i, there):
        def send(n, carry):
            p = peer(n)
            pltpu.make_async_remote_copy(
                src_ref=ps.at[i, p],
                dst_ref=there.at[r],
                send_sem=send2.at[i],
                recv_sem=recv2.at[i],
                device_id=(partner, p),
                device_id_type=MESH,
            ).start()
            return carry

        lax.fori_loop(0, n_rad, send, 0)

    def second(i, carry):
        left(i)
        send_back(i, mv.at[i])
        return carry

    lax.fori_loop(0, kk - 1, second, 0)

    @pl.when(h == 0)
    def _():
        kin[0] = jnp.zeros_like(kin[0])

    @pl.when(h == n_hel - 1)
    def _():
        kin[kk + 1] = jnp.zeros_like(kin[kk + 1])

    def ends(low):
        return (1, kk + 1, 0) if low else (kk, 0, 1)

    def halo(low):
        own, there, n = ends(low)
        return pltpu.make_async_remote_copy(
            src_ref=kin.at[own],
            dst_ref=kin.at[there],
            send_sem=hsend.at[n],
            recv_sem=hrecv.at[n],
            device_id=(h - 1 if low else h + 1, r),
            device_id_type=MESH,
        )

    def quarter(low, q, target, by_helper):
        own, there, n = ends(low)
        rows = pl.ds(q * 512, 512)
        return pltpu.make_async_remote_copy(
            src_ref=kin.at[own, rows],
            dst_ref=relay if by_helper else kin.at[there, rows],
            send_sem=hsend.at[n],
            recv_sem=rrecv if by_helper else hrecv.at[n],
            device_id=(target, r),
            device_id_type=MESH,
        )

    def hand_on(low):
        own, there, n = ends(low)
        q = (h - middle - 1) // 2 if low else (h - 1) // 2
        rows = pl.ds(pl.multiple_of(q * 512, 512), 512)
        return pltpu.make_async_remote_copy(
            src_ref=relay,
            dst_ref=kin.at[there, rows],
            send_sem=rsend,
            recv_sem=hrecv.at[n],
            device_id=(middle - 1 if low else middle, r),
            device_id_type=MESH,
        )

    def arrived_at_helper(low):
        return quarter(low, 0, partner, True)

    def factors(k):
        g = h * kk + k
        row = lax.broadcasted_iota(jnp.int32, (8, 128), 0) % 4
        up, down = jnp.zeros((8, 128), F32), jnp.zeros((8, 128), F32)
        for j in range(4):
            to_up = jnp.where(g < n_hel * kk - 1, coup[j, g], 0.0)
            to_down = jnp.where(g > 0, coup[j, jnp.maximum(g - 1, 0)], 0.0)
            up = jnp.where(row == j, to_up, up)
            down = jnp.where(row == j, to_down, down)
        return up, down

    def at(slot, c, q):
        return tiles(kin[slot, chunk(q, c * 1024)])

    def finish(i):
        phase(mv.at[i], cosv, sinv, ph, 0, 64)
        propagate(ph, pbig, wide, 64)

        def store(q, carry):
            for c in range(2):
                kin[order(i) + 1, chunk(q, c * 1024)] = wide[c, chunk(q)].astype(BF16)
            return carry

        lax.fori_loop(0, 4, store, 0)

    def mix_early():
        k = 3 * z_lo
        up, down = factors(k)

        def block(q, carry):
            w = tiles(wr[chunk(q)])
            by = [w * (up * at(k + 2, c, q) + down * at(k, c, q)) for c in range(2)]
            rows = pl.ds(pl.multiple_of(q * 16, 16), 16)
            for c, x in enumerate((at(k + 1, 0, q) + by[1], at(k + 1, 1, q) - by[0])):
                done[rows, c, k] = flat(x).astype(BF16).reshape(16, 16, 128)
            return carry

        lax.fori_loop(0, 4, block, 0)

    low = 1 - z_lo

    def put_part(n, q, real, imag):
        part[n, 0, chunk(q)] = flat(real)
        part[n, 1, chunk(q)] = flat(imag)

    def part_first():
        up, down = factors(low)

        def block(q, carry):
            w = tiles(wr[chunk(q)])
            by = [w * (down * at(low, c, q)) for c in range(2)]
            put_part(0, q, at(low + 1, 0, q) + by[1], at(low + 1, 1, q) - by[0])
            wu[chunk(q)] = flat(w * up)
            return carry

        lax.fori_loop(0, 4, block, 0)

    def part_middle():
        up, down = factors(low + 1)

        def block(q, carry):
            w = tiles(wr[chunk(q)])
            by = [
                w * (up * at(low + 3, c, q) + down * at(low + 1, c, q))
                for c in range(2)
            ]
            put_part(1, q, by[1], -by[0])
            return carry

        lax.fori_loop(0, 4, block, 0)

    def part_last():
        up, down = factors(low + 2)

        def block(q, carry):
            w = tiles(wr[chunk(q)])
            by = [w * (up * at(low + 4, c, q)) for c in range(2)]
            put_part(2, q, at(low + 3, 0, q) + by[1], at(low + 3, 1, q) - by[0])
            wd[chunk(q)] = flat(w * down)
            return carry

        lax.fori_loop(0, 4, block, 0)

    def third(i):
        all_second(i).wait_recv()
        finish(i)

    def send_edge(low):
        @pl.when((h > 0) & (h != middle) if low else (h < n_hel - 1) & (h != middle - 1))
        def _():
            halo(low).start()

        @pl.when(is_high if low else is_low)
        def _():
            for q in range(4):
                if q == (0 if low else 3):
                    quarter(low, q, middle - 1 if low else middle, False).start()
                else:
                    helper = middle + 2 * q + 1 if low else 2 * q + 1
                    quarter(low, q, helper, True).start()

    on_the_way = is_low | is_high | carries_down | carries_up

    def last_left():
        left(kk - 1)
        for batch, points in enumerate(BATCHES):
            here = pl.ds(*points)

            def send(n, carry):
                p = peer(n)
                pltpu.make_async_remote_copy(
                    src_ref=ps.at[kk - 1, p, here],
                    dst_ref=mvl.at[r, here],
                    send_sem=send2.at[kk - 1 + batch],
                    recv_sem=recv2.at[kk - 1 + batch],
                    device_id=(partner, p),
                    device_id_type=MESH,
                ).start()
                return carry

            lax.fori_loop(0, n_rad, send, 0)

    @pl.when(jnp.logical_not(on_the_way))
    def _():
        last_left()

    third(0)

    @pl.when(z_lo == 1)
    def _():
        send_edge(True)

    @pl.when(z_lo == 0)
    def _():
        send_edge(False)

    @pl.when(carries_down)
    def _():
        arrived_at_helper(True).wait_recv()
        hand_on(True).start()

    @pl.when(carries_up)
    def _():
        arrived_at_helper(False).wait_recv()
        hand_on(False).start()

    @pl.when(on_the_way)
    def _():
        last_left()

    third(1)

    @pl.when(z_lo == 1)
    def _():
        send_edge(False)

    @pl.when(z_lo == 0)
    def _():
        send_edge(True)

    third(2)

    @pl.when((z_lo == 1) & (h < n_hel - 1))
    def _():
        halo(True).wait_recv()

    @pl.when((z_lo == 0) & (h > 0))
    def _():
        halo(False).wait_recv()

    mix_early()
    part_middle()

    @pl.when(z_lo == 1)
    def _():
        part_last()
        halo(False).wait_recv()
        part_first()

    @pl.when(z_lo == 0)
    def _():
        part_first()
        halo(True).wait_recv()
        part_last()

    for batch, (base, count) in enumerate(BATCHES[:-1]):
        all_last(batch).wait_recv()
        phase(mvl, cosv, sinv, ph, base, count)
        propagate(ph, pbig, wide, count)
        for q in range(count // 16):
            combine(q, base, base, low, wide, part, wu, wd, done)
    all_last(len(BATCHES) - 1).wait_recv()

    def drain(i, carry):
        all_first(i).wait_send()
        return carry

    lax.fori_loop(0, kk, drain, 0)

    for i in range(kk - 1):
        all_second(i).wait_send()
    for batch in range(len(BATCHES)):
        all_last(batch).wait_send()

    @pl.when(h > 0)
    def _():
        halo(True).wait_send()

    @pl.when(h < n_hel - 1)
    def _():
        halo(False).wait_send()

    @pl.when(carries_down)
    def _():
        hand_on(True).wait_send()

    @pl.when(carries_up)
    def _():
        hand_on(False).wait_send()


def solution(mesh):
    n_hel, n_rad = mesh.shape["hel"], mesh.shape["rad"]

    def per_device(packet, first, second, potential, coupling, weight):
        hbm = pl.BlockSpec(memory_space=pltpu.HBM)
        vmem = pl.BlockSpec(memory_space=pltpu.VMEM)
        dma = pltpu.SemaphoreType.DMA
        state = pl.pallas_call(
            functools.partial(kernel, n_hel, n_rad),
            out_shape=(
                pltpu.VMEM((64, 2, 4, 16, 128), BF16),
                pltpu.VMEM((1024, 1024), BF16),
                pltpu.VMEM((16, 64, 256), BF16),
                pltpu.VMEM((4, 4, 64, 128), F32),
                pltpu.VMEM((4, 4, 64, 128), F32),
                pltpu.VMEM((3, 2, 1024, 128), F32),
                pltpu.VMEM((1024, 128), F32),
                pltpu.VMEM((1024, 128), F32),
            ),
            in_specs=[hbm] * 6,
            out_specs=[vmem] * 8,
            scratch_shapes=[
                pltpu.VMEM((4, 2, 64, 4, 512), BF16),
                pltpu.VMEM((2, 512, 512), BF16),
                pltpu.VMEM((2, 1024, 1024), BF16),
                pltpu.VMEM((2, 1024, 1024), BF16),
                pltpu.VMEM((64, 4, 512), F32),
                pltpu.VMEM((64, 512), F32),
                pltpu.VMEM((1024, 128), F32),
                pltpu.SMEM((4, 64), F32),
                pltpu.VMEM((8, 256, 128), F32),
                pltpu.VMEM((2, 1024, 128), F32),
                pltpu.VMEM((4, 16, 64, 256), BF16),
                pltpu.VMEM((4, 16, 64, 256), BF16),
                pltpu.VMEM((4, 16, 64, 256), BF16),
                pltpu.VMEM((3, 16, 64, 256), BF16),
                pltpu.VMEM((256, 1024), BF16),
                pltpu.VMEM((6, 2048, 128), BF16),
                pltpu.VMEM((512, 128), BF16),
                dma((5,)),
                dma((4, 2)),
                dma((4,)),
                dma((4,)),
                dma((5,)),
                dma((5,)),
                dma((2,)),
                dma((2,)),
                dma,
                dma,
            ],
            compiler_params=pltpu.CompilerParams(
                collective_id=0,
                has_side_effects=True,
                vmem_limit_bytes=48 * 2**20,
            ),
        )(
            *(
                pltpu.with_memory_space_constraint(a, pltpu.HBM)
                for a in (coupling.T, packet, first, second, potential, weight)
            )
        )
        rows = pl.pallas_call(
            functools.partial(last_rows, n_hel),
            out_shape=pltpu.HBM((64, 2, 4, 16, 128), BF16),
            in_specs=[vmem] * 8,
            out_specs=hbm,
            scratch_shapes=[
                pltpu.VMEM((4 * REST, 1024), BF16),
                pltpu.VMEM((2, REST * 16, 128), F32),
                pltpu.VMEM((REST, 2, 4, 16, 128), BF16),
                dma((4,)),
            ],
            compiler_params=pltpu.CompilerParams(vmem_limit_bytes=16 * 2**20),
        )(*(pltpu.with_memory_space_constraint(a, pltpu.VMEM) for a in state))
        rows = rows.reshape(64, 2, 4, 4, 4, 128)
        return rows.transpose(0, 1, 2, 4, 3, 5).reshape(packet.shape)

    return jax.shard_map(
        per_device,
        mesh=mesh,
        in_specs=(
            P("rad", None, "hel", None, None),
            P(),
            P(),
            P("rad", None, None),
            P(),
            P("rad", None),
        ),
        out_specs=P("rad", None, "hel", None, None),
        check_vma=False,
    )
```
